768 devices in a mesh: seq: 16 (over y, core), head: 48 (over x, z).
Axes of the slice: x: 4, y: 8, z: 12, core: 2. Of those that a mesh axis runs over, the one named last changes fastest.
Arguments:
- query_rows: bfloat16 [6144, 6144], P('seq', 'head'), may hold values from -6 to 6
- key_rows: bfloat16 [8192, 6144], P('seq', 'head'), may hold values from -6 to 6
- value_rows: bfloat16 [8192, 6144], P('seq', 'head'), may hold values from -6 to 6
- attn_out: bfloat16 [6144, 6144], P(('seq', 'head')), may hold values from -3 to 3
- out_grad: bfloat16 [6144, 6144], P(('seq', 'head')), may hold values from -48 to 48
- logsumexp: bfloat16 [48, 6144], P('head', 'seq'), may hold values from 4.5 to 6.5
- shard_pick: int32 [48, 6144, 4], P('head', 'seq'), may hold values from 0 to 15, all different within a row; in each aligned block of 384 rows (0 to 383, 384 to 767, ..., all dimensions but the last counted through in order) at most 192 rows name the same one
- block_pick: int32 [48, 6144, 4, 4], P('head', 'seq'), may hold values from 0 to 7, as said below
Outputs:
- query_grad: bfloat16 [6144, 6144], P('seq', 'head')
- key_grad: bfloat16 [8192, 6144], P('seq', 'head')
- value_grad: bfloat16 [8192, 6144], P('seq', 'head')
The draws below stay inside these ranges and needn't reach their ends.
Inputs may be any that keep to these rules, and one draw needn't show every extreme that they name: `shard_pick`: each query row of each head names 4 different shards; among the 384 rows of one device (one head, one shard of query rows) no shard is named more than 192 times. `block_pick`: the 4 entries of one query row, head and group are different.
All inputs are finite; a program needn't handle non-finite values.
Results may differ from the reference program's by a relative error of at most 0.0077.
Values may be sent and summed in bfloat16 or wider, within the bound.
A program may use at most 32 MiB of HBM per device.

```python
import math
import jax
import jax.numpy as jnp
import numpy as np
from jax import lax

DH = 128
HEADS = 48
BLK = 64
TOPK = 16
GROUPS = 4
PER_GROUP = 4
Q_DEV = 384
QROWS = 6144
KEYS = 8192
BLOCKS_DEV = 8
CAP = 192
N_SEQ = 16


def draw_block_pick(key, part):
    scores = jax.random.randint(key, (HEADS, QROWS, GROUPS, BLOCKS_DEV), 0, 1 << 20, dtype=jnp.int32)
    scores = scores * BLOCKS_DEV + jnp.arange(BLOCKS_DEV, dtype=jnp.int32)
    return lax.top_k(scores, PER_GROUP)[1].astype(jnp.int32)


def shard_levels(stream_key, shape, shards, smallest, high):
    loudness, own = 1.0, jax.random.fold_in(stream_key, 6)
    for dim, shards_of in shards:
        draws = jnp.exp(jax.random.uniform(jax.random.fold_in(own, dim), (shards_of,), jnp.float32, smallest / len(shards), high / len(shards)))
        loudness = loudness * jnp.repeat(draws, shape[dim] // shards_of).reshape([-1 if axis == dim else 1 for axis in range(len(shape))])
    return loudness


def assign_block(key, own, number, rows, count, top, reach, lean):
    sequence = jax.random.permutation(key, count)
    crowded, common = shares(count, rows * top, reach, lean, True), shares(count, rows * top, reach, lean, False)
    places = jnp.arange(count)

    def named(tallies, offset_by):
        used = int((tallies > 0).sum())
        fixed = max(1, used // 4)
        shifted = fixed + (places - fixed + offset_by * (used - fixed)) % max(1, count - fixed)
        return jnp.zeros((count,), jnp.int32).at[sequence[jnp.where(places < fixed, places, shifted)]].set(jnp.asarray(tallies, jnp.int32))

    tallies = jnp.where(number % 4 == 0, named(crowded, number // 4), named(common, number - number // 4 - 1))
    mixed = jax.random.permutation(jax.random.fold_in(own, 3), count)
    source_of, sink = mixed[0:count // 2 * 2:2], mixed[1:count // 2 * 2:2]
    margin = jnp.minimum(tallies[source_of] - 1, reach - tallies[sink]) // 2
    margin = jnp.where((source_of == sequence[0]) | (sink == sequence[0]) | (tallies[sink] == 0), 0, jnp.maximum(margin, 0))
    shifted = jax.random.randint(jax.random.fold_in(own, 4), (count // 2,), 0, 1 << 20) % (margin + 1)
    tallies = tallies.at[source_of].add(-shifted).at[sink].add(shifted)
    items = jnp.searchsorted(jnp.cumsum(tallies), jnp.arange(rows * top), side="right").astype(jnp.int32)
    listing = items.reshape(top, rows).T
    listing = listing[jax.random.permutation(jax.random.fold_in(own, 1), rows)]
    offset_by = jax.random.randint(jax.random.fold_in(own, 2), (rows, 1), 0, top)
    return jnp.take_along_axis(listing, (jnp.arange(top)[None, :] + offset_by) % top, axis=1)


def shares(count, total, reach, skew, full):
    portions = [(1 << 20) // math.isqrt(standing ** skew) + 1 for standing in range(1, count + 1)]
    largest = reach if full else min(reach, max(-(-total // count), total * portions[0] // sum(portions)))
    least = 1 if total - largest >= count - 1 else 0
    holding, spare = [largest] + [least] * (count - 1), total - largest - least * (count - 1)
    while spare > 0:
        candidates = [i for i in range(1, count) if holding[i] < largest] or [i for i in range(1, count) if holding[i] < reach]
        whole, left = sum([portions[i] for i in candidates]), spare
        for i in candidates:
            extra = min(reach - holding[i], max(1, left * portions[i] // whole), spare)
            holding[i] = holding[i] + extra
            spare = spare - extra
    return np.array(holding)


def scatter_about(rng, dims, spread, limit, split=(), kind=jnp.bfloat16):
    loudness = shard_levels(rng, dims, split, -0.22, 0.18) if split else 1.0
    entries = jax.random.normal(rng, dims, jnp.float32) * spread * loudness
    return jnp.minimum(jnp.maximum(entries, -limit), limit).astype(kind)


def setup_inputs(seed: int = 0) -> dict:
    seeds = jax.random.split(jax.random.key(seed), 9)
    query_rows = scatter_about(seeds[0], (QROWS, HEADS * DH), 1.0, 6.0, ((0, 16), (1, 48)))
    key_rows = scatter_about(seeds[1], (KEYS, HEADS * DH), 1.0, 6.0, ((0, 16), (1, 48)))
    value_rows = scatter_about(seeds[2], (KEYS, HEADS * DH), 1.0, 6.0, ((0, 16), (1, 48)))
    attn_out = scatter_about(seeds[3], (QROWS, HEADS * DH), 0.5, 3.0, ((0, 768),))
    out_grad = scatter_about(seeds[4], (QROWS, HEADS * DH), 8.0, 48.0, ((0, 768),))
    logsumexp = jnp.clip(4.5 + 2.0 * jax.random.uniform(seeds[5], (HEADS, QROWS), jnp.float32) ** shard_levels(seeds[5], (HEADS, QROWS), ((0, 48), (1, 16)), -0.2, 0.2), 4.5, 6.5).astype(jnp.bfloat16)
    shard_pick_keys = jax.random.split(jax.random.fold_in(seeds[6], 1), HEADS * QROWS // Q_DEV)
    shard_pick_turns = jax.random.permutation(jax.random.fold_in(seeds[6], 3), HEADS * QROWS // Q_DEV)
    shard_pick = jax.vmap(lambda own, number: assign_block(jax.random.fold_in(seeds[6], 2), own, number, Q_DEV, N_SEQ, GROUPS, CAP, 2))(shard_pick_keys, shard_pick_turns).reshape((HEADS, QROWS, GROUPS))
    block_pick = draw_block_pick(jax.random.fold_in(seeds[8], 71), 0)
    return dict(query_rows=query_rows, key_rows=key_rows, value_rows=value_rows, attn_out=attn_out, out_grad=out_grad, logsumexp=logsumexp, shard_pick=shard_pick, block_pick=block_pick)


def head_grads(pieces):
    q_head, k_head, v_head, g_head, lse_head, delta_head, shard_head, pick_head = pieces
    scale = DH ** -0.5
    blocks = (shard_head[:, :, None] * BLOCKS_DEV + pick_head).reshape(QROWS, TOPK).astype(jnp.int32)
    all_blocks = jnp.arange(N_SEQ * BLOCKS_DEV, dtype=jnp.int32)
    chosen = jnp.any(blocks[:, :, None] == all_blocks[None, None, :], axis=1)
    mask = jnp.repeat(chosen, BLK, axis=1)
    scores = jnp.dot(q_head, k_head.T, preferred_element_type=jnp.float32) * scale
    probs = jnp.where(mask, jnp.exp(scores - lse_head.astype(jnp.float32)[:, None]), jnp.zeros_like(scores))
    probs_low = probs.astype(jnp.bfloat16)
    value_part = jnp.dot(probs_low.T, g_head, preferred_element_type=jnp.float32)
    dprob = jnp.dot(g_head, v_head.T, preferred_element_type=jnp.float32)
    dscore = (probs * (dprob - delta_head.astype(jnp.float32)[:, None])).astype(jnp.bfloat16)
    query_part = jnp.dot(dscore, k_head, preferred_element_type=jnp.float32) * scale
    key_part = jnp.dot(dscore.T, q_head, preferred_element_type=jnp.float32) * scale
    return query_part.astype(jnp.bfloat16), key_part.astype(jnp.bfloat16), value_part.astype(jnp.bfloat16)


def reference(query_rows, key_rows, value_rows, attn_out, out_grad, logsumexp, shard_pick, block_pick):
    delta = (attn_out.astype(jnp.float32) * out_grad.astype(jnp.float32)).reshape(QROWS, HEADS, DH).sum(axis=2)
    delta = lax.optimization_barrier(delta.astype(jnp.bfloat16))
    q_heads = query_rows.reshape(QROWS, HEADS, DH).transpose(1, 0, 2)
    k_heads = key_rows.reshape(KEYS, HEADS, DH).transpose(1, 0, 2)
    v_heads = value_rows.reshape(KEYS, HEADS, DH).transpose(1, 0, 2)
    g_heads = out_grad.reshape(QROWS, HEADS, DH).transpose(1, 0, 2)
    query_grad, key_grad, value_grad = lax.map(head_grads, (q_heads, k_heads, v_heads, g_heads, logsumexp, delta.T, shard_pick, block_pick))
    query_grad = query_grad.transpose(1, 0, 2).reshape(QROWS, HEADS * DH)
    key_grad = key_grad.transpose(1, 0, 2).reshape(KEYS, HEADS * DH)
    value_grad = value_grad.transpose(1, 0, 2).reshape(KEYS, HEADS * DH)
    return query_grad, key_grad, value_grad
```

```python
import functools
import math

import jax
import jax.numpy as jnp
from jax import lax
from jax.experimental import pallas as pl
from jax.experimental.pallas import tpu as pltpu
from jax.sharding import PartitionSpec as P

BLK = 64
RING = 8
LOG2E = math.log2(math.e)
NT = (((1,), (1,)), ((), ()))


def kernel(
    n_head, q_hbm, k_hbm, v_hbm, o_hbm, g_hbm, lse_hbm, sp_hbm, bp_hbm,
    dq_hbm, dk_hbm, dv_hbm,
    qb, gb, kx, vx, kt, o_v, g_v, lse_v, sp_v, bp_v, msg, rcv,
    pt, part, pr, sl, rl, dk_acc, dv_acc, dq_v, dk_v, dv_v,
    in_sem, a2a_send, a2a_recv,
    q_send, q_recv, q_ssend, q_srecv,
    g_send, g_recv, g_ssend, g_srecv,
    p_send, p_recv, c_send, c_recv, out_sem,
):
    rows, dh = q_hbm.shape
    q_rows, g_rows = qb.shape[2], gb.shape[2]
    tiles = rows // 128
    per_shard = kx.shape[0] // BLK
    r = rows // n_head
    half = dh // 2
    own = lax.axis_index("seq")
    head = lax.axis_index("head")
    chip, core = own // 2, own % 2
    right = {"seq": ((chip + 1) % RING) * 2 + core}
    left = {"seq": ((chip + RING - 1) % RING) * 2 + core}
    sib = {"seq": chip * 2 + (1 - core)}
    dirs = (right, left)
    scale = dh ** (-0.5)

    loads = [
        pltpu.make_async_copy(src, dst, in_sem.at[i])
        for i, (src, dst) in enumerate(
            (
                (q_hbm, qb.at[0, 0, pl.ds(0, rows)]),
                (o_hbm, o_v),
                (g_hbm, g_v),
                (lse_hbm, lse_v),
                (sp_hbm, sp_v),
                (bp_hbm, bp_v),
                (k_hbm, kx),
                (v_hbm, vx),
            )
        )
    ]
    for load in loads:
        load.start()

    barrier = pltpu.get_barrier_semaphore()
    for peer in (right, left, sib):
        pl.semaphore_signal(barrier, inc=1, device_id=peer)

    def greet(j, _):
        pl.semaphore_signal(barrier, inc=1, device_id={"head": (head + j) % n_head})
        return 0

    lax.fori_loop(1, n_head, greet, 0)

    for load in loads[:6]:
        load.wait()

    lse = lse_v[...].astype(jnp.float32)
    for t in range(tiles):
        cols = pl.ds(t * 128, 128)
        ids = [sp_v[g : g + 1, cols] * per_shard + bp_v[g, :, cols] for g in range(sp_v.shape[0])]
        ids = jnp.concatenate(ids, axis=0).astype(jnp.float32).astype(jnp.bfloat16)
        qb[0, 0, pl.ds(rows + 16 * t, 16), :] = ids
    sub = lax.broadcasted_iota(jnp.int32, (16, 128), 0)

    def lane_tiles(vec):
        out = jnp.broadcast_to(vec[:, 0:128], (16, 128))
        for t in range(1, tiles):
            out = jnp.where(sub == t, jnp.broadcast_to(vec[:, t * 128 : (t + 1) * 128], (16, 128)), out)
        return out.astype(jnp.bfloat16)

    qb[0, 0, pl.ds(rows + 16 * tiles, 16), :] = lane_tiles(lse)
    for h in range(n_head):
        cols = pl.ds(h * dh, dh)
        msg[h, pl.ds(0, r), :] = g_v[:, cols]
        msg[h, pl.ds(r, r), :] = o_v[:, cols]

    def span(buf, h):
        size = buf.shape[2] // 2 // 16 * 16
        return pl.ds(0, size) if h == 0 else pl.ds(size, buf.shape[2] - size)

    def slot(side, d):
        return d if side == 0 else (RING - d) % RING

    def ring(buf, send, recv, side, d, h):
        return pltpu.make_async_remote_copy(
            src_ref=buf.at[0, slot(side, d), span(buf, h)],
            dst_ref=buf.at[0, slot(side, d + 1), span(buf, h)],
            send_sem=send.at[side, d, h],
            recv_sem=recv.at[side, d + 1, h],
            device_id=dirs[side],
        )

    def ring_arrived(buf, send, recv, side, d, h):
        ring(buf, send, recv, side, d - 1, h).wait_recv()

    def twin(buf, send, recv, k):
        return pltpu.make_async_remote_copy(
            src_ref=buf.at[0, k],
            dst_ref=buf.at[1, k],
            send_sem=send.at[k],
            recv_sem=recv.at[k],
            device_id=sib,
        )

    def start_own(buf, send, recv, ssend, srecv):
        for h in range(2):
            for side in range(2):
                ring(buf, send, recv, side, 0, h).start()
        twin(buf, ssend, srecv, 0).start()

    def relay(buf, send, recv, ssend, srecv, d):
        @pl.when((d >= 1) & (d < 4))
        def _():
            for h in range(2):
                for side in range(2):
                    ring_arrived(buf, send, recv, side, d, h)
                    if h == side:
                        ring(buf, send, recv, side, d, h).start()
                    else:
                        @pl.when(d < 3)
                        def _():
                            ring(buf, send, recv, side, d, h).start()
            for side in range(2):
                twin(buf, ssend, srecv, slot(side, d)).start()

        @pl.when(d == 4)
        def _():
            for side in range(2):
                ring_arrived(buf, send, recv, side, 4, side)
            twin(buf, ssend, srecv, 4).start()

    def drain(buf, send, recv, ssend, srecv):
        def per_distance(d, _):
            for side in range(2):
                for h in range(2):
                    if h == side:
                        ring(buf, send, recv, side, d, h).wait_send()
                    else:
                        @pl.when(d < 3)
                        def _():
                            ring(buf, send, recv, side, d, h).wait_send()
            return 0

        lax.fori_loop(0, 4, per_distance, 0)

        def per_slot(k, _):
            twin(buf, ssend, srecv, k).wait_send()
            return 0

        lax.fori_loop(0, RING, per_slot, 0)

    def visit(d, ssend, srecv, buf, compute):
        def one(j, _):
            par, side = j // 2, j % 2
            k = jnp.where(side == 0, d, (RING - d) % RING)

            @pl.when((side == 0) | ((d >= 1) & (d < 4)))
            def _():
                @pl.when(par == 1)
                def _():
                    twin(buf, ssend, srecv, k).wait_recv()

                compute(par, k)

            return 0

        lax.fori_loop(0, 4, one, 0)

    pl.semaphore_wait(barrier, n_head - 1 + 3)
    q_ring = (qb, q_send, q_recv, q_ssend, q_srecv)
    g_ring = (gb, g_send, g_recv, g_ssend, g_srecv)

    def a2a(j, _):
        peer = (head + j) % n_head
        pltpu.make_async_remote_copy(
            src_ref=msg.at[peer],
            dst_ref=rcv.at[head],
            send_sem=a2a_send,
            recv_sem=a2a_recv,
            device_id={"head": peer},
        ).start()
        return 0

    start_own(*q_ring)
    lax.fori_loop(1, n_head, a2a, 0)
    pltpu.make_async_copy(msg.at[head], rcv.at[head], a2a_recv).start()

    for load in loads[6:]:
        load.wait()
    kt[...] = kx[...].astype(jnp.float32).T.astype(jnp.bfloat16)
    dk_acc[...] = jnp.zeros_like(dk_acc)
    dv_acc[...] = jnp.zeros_like(dv_acc)

    def row_of_tiles(tile):
        return jnp.concatenate([tile[t : t + 1, :] for t in range(tiles)], axis=1)

    def probs(par, k):
        s = lax.dot_general(kx[...], qb[par, k, pl.ds(0, rows), :], NT, preferred_element_type=jnp.float32)
        lse_tile = qb[par, k, pl.ds(rows + 16 * tiles, 16), :].astype(jnp.float32)
        biases = []
        block = lax.broadcasted_iota(jnp.int32, (per_shard, 128), 0)
        for t in range(tiles):
            rel = qb[par, k, pl.ds(rows + 16 * t, 16), :].astype(jnp.float32).astype(jnp.int32) - own * per_shard
            bits = jnp.where((rel >= 0) & (rel < per_shard), jnp.left_shift(1, jnp.maximum(jnp.minimum(rel, per_shard), 0)), 0)
            bits = jnp.sum(bits, axis=0, keepdims=True)
            named = jnp.right_shift(jnp.broadcast_to(bits, (per_shard, 128)), block) & 1
            biases.append(jnp.where(named == 1, jnp.broadcast_to(lse_tile[t : t + 1, :] * -LOG2E, (per_shard, 128)), -1e30))
        bias = jnp.concatenate(biases, axis=1)
        for b in range(per_shard):
            pt[par, k, pl.ds(b * BLK, BLK), :] = jnp.exp2(
                s[b * BLK : (b + 1) * BLK, :] * (scale * LOG2E) + bias[b : b + 1, :]
            )

    def grads(par, k):
        g = gb[par, k, pl.ds(0, rows), :]
        delta = row_of_tiles(gb[par, k, pl.ds(rows, 16), :].astype(jnp.float32))
        dp = lax.dot_general(vx[...], g, NT, preferred_element_type=jnp.float32)
        p = pt[par, k]
        ds = (p * (dp - delta)).astype(jnp.bfloat16)
        dv_acc[...] += jnp.dot(p.astype(jnp.bfloat16), g, preferred_element_type=jnp.float32)
        dk_acc[...] += jnp.dot(ds, qb[par, k, pl.ds(0, rows), :], preferred_element_type=jnp.float32)
        part[par, k] = jnp.dot(kt[...], ds, preferred_element_type=jnp.float32)

        @pl.when(par == 1)
        def _():
            give(k).start()

    def give(k):
        return pltpu.make_async_remote_copy(
            src_ref=part.at[1, k],
            dst_ref=pr.at[k],
            send_sem=p_send.at[k],
            recv_sem=p_recv.at[k],
            device_id=sib,
        )

    def gather_grad():
        pltpu.make_async_copy(rcv, rcv, a2a_recv).wait()
        both = rcv[...].astype(jnp.float32)
        g = both[:, 0:r, :].reshape(rows, dh)
        o = both[:, r : 2 * r, :].reshape(rows, dh)
        delta = lax.dot_general(
            jnp.ones((8, dh), jnp.float32), g * o, NT,
            precision=lax.Precision.HIGHEST, preferred_element_type=jnp.float32,
        )
        gb[0, 0, pl.ds(0, rows), :] = g.astype(jnp.bfloat16)
        gb[0, 0, pl.ds(rows, 16), :] = lane_tiles(delta[0:1, :])
        start_own(*g_ring)

    def q_step(d, _):
        relay(*q_ring, d)

        @pl.when(d == 2)
        def _():
            gather_grad()

        visit(d, q_ssend, q_srecv, qb, probs)
        return 0

    lax.fori_loop(0, 5, q_step, 0)

    def chain(side, d, h):
        return pltpu.make_async_remote_copy(
            src_ref=sl.at[side, d, h],
            dst_ref=rl.at[side, d - 1, h],
            send_sem=c_send.at[side, d, h],
            recv_sem=c_recv.at[side, d - 1, h],
            device_id=dirs[1 - side],
        )

    def local_sum(k, h):
        return part[0, k, pl.ds(h * half, half), :] + pr[k, pl.ds(h * half, half), :]

    def send_home(side, d, h, first):
        total = local_sum(slot(side, d), h)
        if not first:
            chain(side, d + 1, h).wait_recv()
            total = total + rl[side, d, h].astype(jnp.float32)
        sl[side, d, h] = total.astype(jnp.bfloat16)
        chain(side, d, h).start()

    def g_step(d, _):
        @pl.when(d == 4)
        def _():
            for k in (3, 5):
                give(k).wait_recv()
            send_home(0, 3, 1, True)
            send_home(1, 3, 0, True)

        relay(*g_ring, d)
        visit(d, g_ssend, g_srecv, gb, grads)
        return 0

    lax.fori_loop(0, 5, g_step, 0)

    for k in (0, 1, 2, 4, 6, 7):
        give(k).wait_recv()
    send_home(0, 4, 0, True)
    send_home(1, 4, 1, True)

    dk_v[...] = (dk_acc[...] * scale).astype(jnp.bfloat16)
    dv_v[...] = dv_acc[...].astype(jnp.bfloat16)
    stores = [
        pltpu.make_async_copy(dk_v, dk_hbm, out_sem.at[0]),
        pltpu.make_async_copy(dv_v, dv_hbm, out_sem.at[1]),
    ]
    for store in stores:
        store.start()

    for d in (2, 1):
        send_home(0, d, 1, False)
        send_home(1, d, 0, False)
        send_home(0, d + 1, 0, False)
        send_home(1, d + 1, 1, False)
    send_home(0, 1, 0, False)
    send_home(1, 1, 1, False)
    for h in range(2):
        total = local_sum(0, h)
        for side in range(2):
            chain(side, 1, h).wait_recv()
            total = total + rl[side, 0, h].astype(jnp.float32)
        dq_v[:, pl.ds(h * half, half)] = (total * scale).T.astype(jnp.bfloat16)
    stores.append(pltpu.make_async_copy(dq_v, dq_hbm, out_sem.at[2]))
    stores[2].start()

    drain(*q_ring)
    drain(*g_ring)

    def given(k, _):
        give(k).wait_send()
        return 0

    lax.fori_loop(0, RING, given, 0)
    for side in range(2):
        for d in range(1, 5):
            for h in range(2):
                if d < 4 or h == side:
                    chain(side, d, h).wait_send()
    if n_head > 1:
        others = msg.at[pl.ds(0, n_head - 1)]
        pltpu.make_async_copy(others, others, a2a_send).wait()
    for store in stores:
        store.wait()


def local(query_rows, key_rows, value_rows, attn_out, out_grad, logsumexp, shard_pick, block_pick):
    n_head = lax.axis_size("head")
    rows, dh = query_rows.shape
    keys = key_rows.shape[0]
    r = rows // n_head
    tiles = rows // 128
    q_rows = rows + 16 * tiles + 16
    g_rows = rows + 16
    groups, per_group = block_pick.shape[2:]
    bf, f32 = jnp.bfloat16, jnp.float32
    dma = pltpu.SemaphoreType.DMA
    vm = pltpu.VMEM
    return pl.pallas_call(
        functools.partial(kernel, n_head),
        out_shape=(
            jax.ShapeDtypeStruct((rows, dh), bf),
            jax.ShapeDtypeStruct((keys, dh), bf),
            jax.ShapeDtypeStruct((keys, dh), bf),
        ),
        in_specs=[pl.BlockSpec(memory_space=pl.ANY)] * 8,
        out_specs=(pl.BlockSpec(memory_space=pl.ANY),) * 3,
        scratch_shapes=[
            vm((2, RING, q_rows, dh), bf),
            vm((2, RING, g_rows, dh), bf),
            vm((keys, dh), bf),
            vm((keys, dh), bf),
            vm((dh, keys), bf),
            vm((r, n_head * dh), bf),
            vm((r, n_head * dh), bf),
            vm((1, rows), bf),
            vm((groups, rows), jnp.int32),
            vm((groups, per_group, rows), jnp.int32),
            vm((n_head, 2 * r, dh), bf),
            vm((n_head, 2 * r, dh), bf),
            vm((2, RING, keys, rows), f32),
            vm((2, RING, dh, rows), f32),
            vm((RING, dh, rows), f32),
            vm((2, 5, 2, dh // 2, rows), bf),
            vm((2, 4, 2, dh // 2, rows), bf),
            vm((keys, dh), f32),
            vm((keys, dh), f32),
            vm((rows, dh), bf),
            vm((keys, dh), bf),
            vm((keys, dh), bf),
            dma((8,)),
            dma,
            dma,
            dma((2, 4, 2)), dma((2, 5, 2)), dma((RING,)), dma((RING,)),
            dma((2, 4, 2)), dma((2, 5, 2)), dma((RING,)), dma((RING,)),
            dma((RING,)), dma((RING,)), dma((2, 5, 2)), dma((2, 4, 2)),
            dma((3,)),
        ],
        compiler_params=pltpu.CompilerParams(
            collective_id=0, has_side_effects=True, vmem_limit_bytes=56 << 20
        ),
        name="sparse_bwd",
    )(
        query_rows, key_rows, value_rows, attn_out, out_grad, logsumexp,
        shard_pick[0].T, block_pick[0].transpose(1, 2, 0),
    )


def solution(mesh):
    placed = (
        P("seq", "head"),
        P("seq", "head"),
        P("seq", "head"),
        P(("seq", "head"), None),
        P(("seq", "head"), None),
        P("head", "seq"),
        P("head", "seq", None),
        P("head", "seq", None, None),
    )
    return jax.shard_map(
        local,
        mesh=mesh,
        in_specs=placed,
        out_specs=(P("seq", "head"), P("seq", "head"), P("seq", "head")),
        check_vma=False,
    )
```

```python
import functools
import math

import jax
import jax.numpy as jnp
from jax import lax
from jax.experimental import pallas as pl
from jax.experimental.pallas import tpu as pltpu
from jax.sharding import PartitionSpec as P

BLK = 64
RING = 8
HEAD_Z = 12
PIECES = 2
CHAIN = 4
LOG2E = math.log2(math.e)
NT = (((1,), (1,)), ((), ()))


def kernel(
    n_head, q_hbm, k_hbm, v_hbm, o_hbm, g_hbm, lse_hbm, sp_hbm, bp_hbm,
    dq_hbm, dk_hbm, dv_hbm,
    qb, gb, db, kx, vx, kt, o_v, g_v, lse_v, sp_v, bp_v, got_g, got_o,
    pt, part, pr, sl, rl, far_s, far_r, dk_acc, dv_acc, dq_v, dk_v, dv_v,
    in_sem, ga_send, ga_recv, oa_send, oa_recv,
    q_send, q_recv, q_ssend, q_srecv,
    g_send, g_recv, g_ssend, g_srecv,
    d_send, d_recv, d_ssend, d_srecv,
    p_send, p_recv, c_send, c_recv, f_send, f_recv, out_sem,
):
    rows, dh = q_hbm.shape
    tiles = rows // 128
    per_shard = kx.shape[0] // BLK
    r = rows // n_head
    own = lax.axis_index("seq")
    head = lax.axis_index("head")
    chip, core = own // 2, own % 2

    def at_chip(offset):
        return {"seq": ((chip + offset + RING) % RING) * 2 + core}

    right, left = at_chip(1), at_chip(-1)
    sib = {"seq": chip * 2 + (1 - core)}
    dirs = (right, left)
    far_home = (at_chip(-3), at_chip(3))
    scale = dh ** (-0.5)

    zn = HEAD_Z if n_head % HEAD_Z == 0 else n_head
    xn = n_head // zn

    my_x, my_z = head // zn, head % zn

    def away(n, i):
        m = (i + 1) // 2
        return (n // 2 + (2 * (i % 2) - 1) * m + n) % n

    def moved(at, by, n):
        if by == 0:
            return at
        at = at + by
        return jnp.where(at >= n, at - n, at)

    peer_z = [moved(my_z, away(zn, i), zn) for i in range(zn)]
    peer_x = [moved(my_x, away(xn, i), xn) * zn for i in range(xn)]
    peers = [x + z for z in peer_z for x in peer_x][: n_head - 1]

    barrier = pltpu.get_barrier_semaphore()
    for peer in peers:
        pl.semaphore_signal(barrier, inc=1, device_id={"head": peer})
    for peer in (right, left, sib) + far_home:
        pl.semaphore_signal(barrier, inc=1, device_id=peer)

    loads = [
        pltpu.make_async_copy(src, dst, in_sem.at[i])
        for i, (src, dst) in enumerate(
            (
                (q_hbm, qb.at[0, 0, pl.ds(0, rows)]),
                (lse_hbm, lse_v),
                (sp_hbm, sp_v),
                (bp_hbm, bp_v),
                (g_hbm, g_v),
                (o_hbm, o_v),
                (k_hbm, kx),
                (v_hbm, vx),
            )
        )
    ]
    for load in loads:
        load.start()

    for load in loads[:4]:
        load.wait()

    lse = lse_v[...].astype(jnp.float32)
    for t in range(tiles):
        cols = pl.ds(t * 128, 128)
        ids = [sp_v[g : g + 1, cols] * per_shard + bp_v[g, :, cols] for g in range(sp_v.shape[0])]
        ids = jnp.concatenate(ids, axis=0).astype(jnp.float32).astype(jnp.bfloat16)
        qb[0, 0, pl.ds(rows + 16 * t, 16), :] = ids
    sub = lax.broadcasted_iota(jnp.int32, (16, 128), 0)

    def lane_tiles(vec):
        out = jnp.broadcast_to(vec[:, 0:128], (16, 128))
        for t in range(1, tiles):
            out = jnp.where(sub == t, jnp.broadcast_to(vec[:, t * 128 : (t + 1) * 128], (16, 128)), out)
        return out.astype(jnp.bfloat16)

    qb[0, 0, pl.ds(rows + 16 * tiles, 16), :] = lane_tiles(lse)
    for load in loads[4:6]:
        load.wait()

    def slot(side, d):
        return d if side == 0 else (RING - d) % RING

    class Ring:
        def __init__(self, buf, pieces, send, recv, ssend, srecv):
            self.buf, self.pieces = buf, pieces
            self.send, self.recv, self.ssend, self.srecv = send, recv, ssend, srecv
            self.size = buf.shape[2] // pieces

        def hop(self, side, d, h):
            span = pl.ds(pl.multiple_of(h * self.size, 8), self.size)
            return pltpu.make_async_remote_copy(
                src_ref=self.buf.at[0, slot(side, d), span],
                dst_ref=self.buf.at[0, slot(side, d + 1), span],
                send_sem=self.send.at[side, d, h],
                recv_sem=self.recv.at[side, d + 1, h],
                device_id=dirs[side],
            )

        def twin(self, k):
            return pltpu.make_async_remote_copy(
                src_ref=self.buf.at[0, k],
                dst_ref=self.buf.at[1, k],
                send_sem=self.ssend.at[k],
                recv_sem=self.srecv.at[k],
                device_id=sib,
            )

        def order(self, side, i):
            return (i + side * (self.pieces // 2)) % self.pieces

        def last_hop(self, side, i):
            return i < self.pieces // 2 if self.pieces > 1 else side == 0

        def start_own(self):
            for i in range(self.pieces):
                for side in range(2):
                    self.hop(side, 0, self.order(side, i)).start()
            self.twin(0).start()

        def relay(self, d):
            def one(i, _):
                self.relay_piece(d, i)
                return 0

            lax.fori_loop(0, self.pieces, one, 0)
            self.twin(d).start()

            @pl.when(d < 4)
            def _():
                self.twin(RING - d).start()

        def relay_piece(self, d, i):
            for side in range(2):
                h = self.order(side, i)

                @pl.when((d < 4) | self.last_hop(side, i))
                def _():
                    self.hop(side, d - 1, h).wait_recv()

                @pl.when((d < 3) | ((d == 3) & self.last_hop(side, i)))
                def _():
                    self.hop(side, d, h).start()

        def drain(self):
            def per_hop(d, _):
                def per_piece(i, _):
                    for side in range(2):
                        @pl.when((d < 3) | self.last_hop(side, i))
                        def _():
                            self.hop(side, d, self.order(side, i)).wait_send()
                    return 0

                return lax.fori_loop(0, self.pieces, per_piece, 0)

            lax.fori_loop(0, 4, per_hop, 0)

            def per_slot(k, _):
                self.twin(k).wait_send()
                return 0

            lax.fori_loop(0, RING, per_slot, 0)

    q_ring = Ring(qb, PIECES, q_send, q_recv, q_ssend, q_srecv)
    g_ring = Ring(gb, PIECES, g_send, g_recv, g_ssend, g_srecv)
    d_ring = Ring(db, 1, d_send, d_recv, d_ssend, d_srecv)

    def to_head(src, dst, send, recv, some):
        for peer in some:
            pltpu.make_async_remote_copy(
                src_ref=src.at[:, pl.ds(pl.multiple_of(peer * dh, dh), dh)],
                dst_ref=dst.at[head],
                send_sem=send,
                recv_sem=recv,
                device_id={"head": peer},
            ).start()

    def to_self(src, dst, recv):
        mine = src.at[:, pl.ds(pl.multiple_of(head * dh, dh), dh)]
        pltpu.make_async_copy(mine, dst.at[head], recv).start()

    pl.semaphore_wait(barrier, n_head - 1 + 5)
    to_head(g_v, got_g, ga_send, ga_recv, peers)
    to_self(g_v, got_g, ga_recv)
    q_ring.start_own()
    to_head(o_v, got_o, oa_send, oa_recv, peers)
    to_self(o_v, got_o, oa_recv)

    for load in loads[6:]:
        load.wait()

    def probs(par, k):
        s = lax.dot_general(kx[...], qb[par, k, pl.ds(0, rows), :], NT, preferred_element_type=jnp.float32)
        lse_tile = qb[par, k, pl.ds(rows + 16 * tiles, 16), :].astype(jnp.float32)
        biases = []
        block = lax.broadcasted_iota(jnp.int32, (per_shard, 128), 0)
        for t in range(tiles):
            rel = qb[par, k, pl.ds(rows + 16 * t, 16), :].astype(jnp.float32).astype(jnp.int32) - own * per_shard
            bits = jnp.where((rel >= 0) & (rel < per_shard), jnp.left_shift(1, jnp.maximum(jnp.minimum(rel, per_shard), 0)), 0)
            bits = jnp.sum(bits, axis=0, keepdims=True)
            named = jnp.right_shift(jnp.broadcast_to(bits, (per_shard, 128)), block) & 1
            biases.append(jnp.where(named == 1, jnp.broadcast_to(lse_tile[t : t + 1, :] * -LOG2E, (per_shard, 128)), -1e30))
        bias = jnp.concatenate(biases, axis=1)
        for b in range(per_shard):
            pt[par, k, pl.ds(b * BLK, BLK), :] = jnp.exp2(
                s[b * BLK : (b + 1) * BLK, :] * (scale * LOG2E) + bias[b : b + 1, :]
            )

    def give(k):
        return pltpu.make_async_remote_copy(
            src_ref=part.at[1, k],
            dst_ref=pr.at[k],
            send_sem=p_send.at[k],
            recv_sem=p_recv.at[k],
            device_id=sib,
        )

    def grads(par, k):
        g = gb[par, k]
        tile = db[par, k].astype(jnp.float32)
        delta = jnp.concatenate([tile[t : t + 1, :] for t in range(tiles)], axis=1)
        dp = lax.dot_general(vx[...], g, NT, preferred_element_type=jnp.float32)
        p = pt[par, k]
        ds = (p * (dp - delta)).astype(jnp.bfloat16)
        part[par, k] = jnp.dot(kt[...], ds, preferred_element_type=jnp.float32)

        @pl.when(par == 1)
        def _():
            give(k).start()

        dv_acc[...] += jnp.dot(p.astype(jnp.bfloat16), g, preferred_element_type=jnp.float32)
        dk_acc[...] += jnp.dot(ds, qb[par, k, pl.ds(0, rows), :], preferred_element_type=jnp.float32)

    def visit(d, par, side, rings, compute):
        k = jnp.where(side == 0, d, (RING - d) % RING)

        @pl.when(((side == 0) & (d >= 0) & (d <= 4)) | ((d >= 1) & (d < 4)))
        def _():
            @pl.when(par == 1)
            def _():
                for ring in rings:
                    ring.twin(k).wait_recv()

            compute(par, k)

    width = dh // CHAIN

    def chain(side, d, h):
        return pltpu.make_async_remote_copy(
            src_ref=sl.at[side, d, h],
            dst_ref=rl.at[side, d - 1, h],
            send_sem=c_send.at[side, d, h],
            recv_sem=c_recv.at[side, d - 1, h],
            device_id=dirs[1 - side],
        )

    def far(side):
        return pltpu.make_async_remote_copy(
            src_ref=far_s.at[side],
            dst_ref=far_r.at[side],
            send_sem=f_send.at[side],
            recv_sem=f_recv.at[side],
            device_id=far_home[side],
        )

    def local_sum(k, h):
        return part[0, k, pl.ds(h * width, width), :] + pr[k, pl.ds(h * width, width), :]

    def mine_to_take(side, h):
        return (h < CHAIN // 2) == (side == 0)

    def send_home(d):
        for side in range(2):
            give(slot(side, d)).wait_recv()
        for i in range(CHAIN):
            for side in range(2):
                h = (i + (1 - side) * (CHAIN // 2)) % CHAIN
                total = local_sum(slot(side, d), h)
                if d < 3:
                    chain(side, d + 1, h).wait_recv()
                    total = total + rl[side, d, h].astype(jnp.float32)
                if d == 1 and mine_to_take(side, h):
                    if i == CHAIN // 2:
                        far(side).wait_recv()
                    total = total + far_r[side, i - CHAIN // 2].astype(jnp.float32)
                sl[side, d, h] = total.astype(jnp.bfloat16)
                chain(side, d, h).start()

    def tick(t, _):
        @pl.when((t >= 1) & (t <= 4))
        def _():
            q_ring.relay(t)

        def forward(j, _):
            visit(t, j // 2, j % 2, (q_ring,), probs)
            return 0

        @pl.when(t <= 4)
        def _():
            lax.fori_loop(0, 4, forward, 0)

        @pl.when(t == 2)
        def _():
            pltpu.make_async_copy(got_g, got_g, ga_recv).wait()
            g = got_g[...].astype(jnp.float32).reshape(rows, dh)
            gb[0, 0] = g.astype(jnp.bfloat16)
            g_ring.start_own()
            kt[...] = kx[...].astype(jnp.float32).T.astype(jnp.bfloat16)
            dk_acc[...] = jnp.zeros_like(dk_acc)
            dv_acc[...] = jnp.zeros_like(dv_acc)
            pltpu.make_async_copy(got_o, got_o, oa_recv).wait()
            o = got_o[...].astype(jnp.float32).reshape(rows, dh)
            delta = lax.dot_general(
                jnp.ones((8, dh), jnp.float32), gb[0, 0].astype(jnp.float32) * o, NT,
                precision=lax.Precision.HIGHEST, preferred_element_type=jnp.float32,
            )
            db[0, 0] = lane_tiles(delta[0:1, :])
            d_ring.start_own()

        @pl.when(t >= 3)
        def _():
            g_ring.relay(t - 2)
            d_ring.relay(t - 2)

        def backward(j, _):
            visit(t - 2, j // 2, j % 2, (g_ring, d_ring), grads)

            @pl.when((t == 6) & (j == 1))
            def _():
                send_home(3)

            return 0

        @pl.when(t >= 2)
        def _():
            lax.fori_loop(0, 4, backward, 0)

        return 0

    lax.fori_loop(0, 7, tick, 0)

    give(4).wait_recv()
    for side in range(2):
        for i in range(CHAIN // 2):
            far_s[side, i] = local_sum(4, side * (CHAIN // 2) + i).astype(jnp.bfloat16)
        far(side).start()

    dk_v[...] = (dk_acc[...] * scale).astype(jnp.bfloat16)
    dv_v[...] = dv_acc[...].astype(jnp.bfloat16)
    stores = [
        pltpu.make_async_copy(dk_v, dk_hbm, out_sem.at[0]),
        pltpu.make_async_copy(dv_v, dv_hbm, out_sem.at[1]),
        pltpu.make_async_copy(dq_v, dq_hbm, out_sem.at[2]),
    ]
    stores[0].start()
    stores[1].start()

    send_home(2)
    send_home(1)
    give(0).wait_recv()
    totals = []
    for h in range(CHAIN):
        total = local_sum(0, h)
        for side in range(2):
            chain(side, 1, h).wait_recv()
            total = total + rl[side, 0, h].astype(jnp.float32)
        totals.append(total)
    dq_v[...] = (jnp.concatenate(totals, axis=0) * scale).T.astype(jnp.bfloat16)
    stores[2].start()

    q_ring.drain()
    g_ring.drain()
    d_ring.drain()

    def given(k, _):
        give(k).wait_send()
        return 0

    lax.fori_loop(0, RING, given, 0)
    for side in range(2):
        far(side).wait_send()
        for d in range(1, 4):
            for h in range(CHAIN):
                chain(side, d, h).wait_send()
    if n_head > 1:
        for got, sem in ((got_g, ga_send), (got_o, oa_send)):
            others = got.at[pl.ds(0, n_head - 1)]
            pltpu.make_async_copy(others, others, sem).wait()
    for store in stores:
        store.wait()


def local(query_rows, key_rows, value_rows, attn_out, out_grad, logsumexp, shard_pick, block_pick):
    n_head = lax.axis_size("head")
    rows, dh = query_rows.shape
    keys = key_rows.shape[0]
    r = rows // n_head
    tiles = rows // 128
    q_rows = rows + 16 * tiles + 16
    groups, per_group = block_pick.shape[2:]
    bf, f32 = jnp.bfloat16, jnp.float32
    dma = pltpu.SemaphoreType.DMA
    vm = pltpu.VMEM
    return pl.pallas_call(
        functools.partial(kernel, n_head),
        out_shape=(
            jax.ShapeDtypeStruct((rows, dh), bf),
            jax.ShapeDtypeStruct((keys, dh), bf),
            jax.ShapeDtypeStruct((keys, dh), bf),
        ),
        in_specs=[pl.BlockSpec(memory_space=pl.ANY)] * 8,
        out_specs=(pl.BlockSpec(memory_space=pl.ANY),) * 3,
        scratch_shapes=[
            vm((2, RING, q_rows, dh), bf),
            vm((2, RING, rows, dh), bf),
            vm((2, RING, 16, dh), bf),
            vm((keys, dh), bf),
            vm((keys, dh), bf),
            vm((dh, keys), bf),
            vm((r, n_head * dh), bf),
            vm((r, n_head * dh), bf),
            vm((1, rows), bf),
            vm((groups, rows), jnp.int32),
            vm((groups, per_group, rows), jnp.int32),
            vm((n_head, r, dh), bf),
            vm((n_head, r, dh), bf),
            vm((2, RING, keys, rows), f32),
            vm((2, RING, dh, rows), f32),
            vm((RING, dh, rows), f32),
            vm((2, 4, CHAIN, dh // CHAIN, rows), bf),
            vm((2, 3, CHAIN, dh // CHAIN, rows), bf),
            vm((2, CHAIN // 2, dh // CHAIN, rows), bf),
            vm((2, CHAIN // 2, dh // CHAIN, rows), bf),
            vm((keys, dh), f32),
            vm((keys, dh), f32),
            vm((rows, dh), bf),
            vm((keys, dh), bf),
            vm((keys, dh), bf),
            dma((8,)),
            dma, dma, dma, dma,
            dma((2, 4, PIECES)), dma((2, 5, PIECES)), dma((RING,)), dma((RING,)),
            dma((2, 4, PIECES)), dma((2, 5, PIECES)), dma((RING,)), dma((RING,)),
            dma((2, 4, 1)), dma((2, 5, 1)), dma((RING,)), dma((RING,)),
            dma((RING,)), dma((RING,)), dma((2, 4, CHAIN)), dma((2, 3, CHAIN)),
            dma((2,)), dma((2,)), dma((3,)),
        ],
        compiler_params=pltpu.CompilerParams(
            collective_id=0, has_side_effects=True, vmem_limit_bytes=56 << 20
        ),
        name="sparse_bwd",
    )(
        query_rows, key_rows, value_rows, attn_out, out_grad, logsumexp,
        shard_pick[0].T, block_pick[0].transpose(1, 2, 0),
    )


def solution(mesh):
    placed = (
        P("seq", "head"),
        P("seq", "head"),
        P("seq", "head"),
        P(("seq", "head"), None),
        P(("seq", "head"), None),
        P("head", "seq"),
        P("head", "seq", None),
        P("head", "seq", None, None),
    )
    return jax.shard_map(
        local,
        mesh=mesh,
        in_specs=placed,
        out_specs=(P("seq", "head"), P("seq", "head"), P("seq", "head")),
        check_vma=False,
    )
```

```python
import functools
import math

import jax
import jax.numpy as jnp
from jax import lax
from jax.experimental import pallas as pl
from jax.experimental.pallas import tpu as pltpu
from jax.sharding import PartitionSpec as P

BLK = 64
RING = 8
HEAD_Z = 12
CHAIN = 4
LOG2E = math.log2(math.e)
NT = (((1,), (1,)), ((), ()))


def kernel(
    n_head, q_hbm, k_hbm, v_hbm, o_hbm, g_hbm, lse_hbm, sp_hbm, bp_hbm,
    dq_hbm, dk_hbm, dv_hbm,
    qb, gb, kx, vx, kt, o_v, g_v, lse_v, sp_v, bp_v, got_g, got_o,
    pt, part, pr, sl, rl, far_s, far_r, dk_acc, dv_acc, dq_v, dk_v, dv_v,
    in_sem, ga_send, ga_recv, oa_send, oa_recv,
    q_send, q_recv, q_ssend, q_srecv,
    g_send, g_recv, g_ssend, g_srecv,
    p_send, p_recv, c_send, c_recv, f_send, f_recv, out_sem,
):
    rows, dh = q_hbm.shape
    tiles = rows // 128
    per_shard = kx.shape[0] // BLK
    r = rows // n_head
    own = lax.axis_index("seq")
    head = lax.axis_index("head")
    chip, core = own // 2, own % 2

    def at_chip(offset):
        return {"seq": ((chip + offset + RING) % RING) * 2 + core}

    right, left = at_chip(1), at_chip(-1)
    sib = {"seq": chip * 2 + (1 - core)}
    dirs = (right, left)
    far_home = (at_chip(-3), at_chip(3))
    scale = dh ** (-0.5)

    zn = HEAD_Z if n_head % HEAD_Z == 0 else n_head
    xn = n_head // zn

    my_x, my_z = head // zn, head % zn

    def away(n, i):
        m = (i + 1) // 2
        return (n // 2 + (2 * (i % 2) - 1) * m + n) % n

    def moved(at, by, n):
        if by == 0:
            return at
        at = at + by
        return jnp.where(at >= n, at - n, at)

    peer_z = [moved(my_z, away(zn, i), zn) for i in range(zn)]
    peer_x = [moved(my_x, away(xn, i), xn) * zn for i in range(xn)]
    peers = [x + z for z in peer_z for x in peer_x][: n_head - 1]

    barrier = pltpu.get_barrier_semaphore()
    for peer in peers:
        pl.semaphore_signal(barrier, inc=1, device_id={"head": peer})
    for peer in (right, left, sib) + far_home:
        pl.semaphore_signal(barrier, inc=1, device_id=peer)

    loads = [
        pltpu.make_async_copy(src, dst, in_sem.at[i])
        for i, (src, dst) in enumerate(
            (
                (q_hbm, qb.at[0, 0, pl.ds(0, rows)]),
                (lse_hbm, lse_v),
                (sp_hbm, sp_v),
                (bp_hbm, bp_v),
                (g_hbm, g_v),
                (o_hbm, o_v),
                (k_hbm, kx),
                (v_hbm, vx),
            )
        )
    ]
    for load in loads:
        load.start()

    for load in loads[:4]:
        load.wait()

    lse = lse_v[...].astype(jnp.float32)
    for t in range(tiles):
        cols = pl.ds(t * 128, 128)
        ids = [sp_v[g : g + 1, cols] * per_shard + bp_v[g, :, cols] for g in range(sp_v.shape[0])]
        ids = jnp.concatenate(ids, axis=0).astype(jnp.float32).astype(jnp.bfloat16)
        qb[0, 0, pl.ds(rows + 16 * t, 16), :] = ids
    sub = lax.broadcasted_iota(jnp.int32, (16, 128), 0)

    def lane_tiles(vec):
        out = jnp.broadcast_to(vec[:, 0:128], (16, 128))
        for t in range(1, tiles):
            out = jnp.where(sub == t, jnp.broadcast_to(vec[:, t * 128 : (t + 1) * 128], (16, 128)), out)
        return out.astype(jnp.bfloat16)

    qb[0, 0, pl.ds(rows + 16 * tiles, 16), :] = lane_tiles(lse)
    for load in loads[4:6]:
        load.wait()

    def slot(side, d):
        return d if side == 0 else (RING - d) % RING

    class Ring:
        def __init__(self, buf, cut, send, recv, ssend, srecv):
            self.buf = buf
            self.spans = (pl.ds(0, cut), pl.ds(cut, buf.shape[2] - cut))
            self.send, self.recv, self.ssend, self.srecv = send, recv, ssend, srecv

        def hop(self, side, d, h):
            return pltpu.make_async_remote_copy(
                src_ref=self.buf.at[0, slot(side, d), self.spans[h]],
                dst_ref=self.buf.at[0, slot(side, d + 1), self.spans[h]],
                send_sem=self.send.at[side, d, h],
                recv_sem=self.recv.at[side, d + 1, h],
                device_id=dirs[side],
            )

        def twin(self, k):
            return pltpu.make_async_remote_copy(
                src_ref=self.buf.at[0, k],
                dst_ref=self.buf.at[1, k],
                send_sem=self.ssend.at[k],
                recv_sem=self.srecv.at[k],
                device_id=sib,
            )

        def start_piece(self, h):
            for side in range(2):
                self.hop(side, 0, h).start()

        def relay(self, d):
            for h in range(2):
                for side in range(2):
                    @pl.when((d < 4) | (h == side))
                    def _():
                        self.hop(side, d - 1, h).wait_recv()

                    @pl.when((d < 3) | ((d == 3) & (h == side)))
                    def _():
                        self.hop(side, d, h).start()

            self.twin(d).start()

            @pl.when(d < 4)
            def _():
                self.twin(RING - d).start()

        def drain(self):
            def per_hop(d, _):
                for h in range(2):
                    for side in range(2):
                        @pl.when((d < 3) | (h == side))
                        def _():
                            self.hop(side, d, h).wait_send()
                return 0

            lax.fori_loop(0, 4, per_hop, 0)

            def per_slot(k, _):
                self.twin(k).wait_send()
                return 0

            lax.fori_loop(0, RING, per_slot, 0)

    q_ring = Ring(qb, qb.shape[2] // 2, q_send, q_recv, q_ssend, q_srecv)
    g_ring = Ring(gb, rows // 2, g_send, g_recv, g_ssend, g_srecv)

    def to_head(src, dst, send, recv, some):
        for peer in some:
            pltpu.make_async_remote_copy(
                src_ref=src.at[:, pl.ds(pl.multiple_of(peer * dh, dh), dh)],
                dst_ref=dst.at[head],
                send_sem=send,
                recv_sem=recv,
                device_id={"head": peer},
            ).start()

    def to_self(src, dst, recv):
        mine = src.at[:, pl.ds(pl.multiple_of(head * dh, dh), dh)]
        pltpu.make_async_copy(mine, dst.at[head], recv).start()

    pl.semaphore_wait(barrier, n_head - 1 + 5)
    to_head(g_v, got_g, ga_send, ga_recv, peers)
    to_self(g_v, got_g, ga_recv)
    q_ring.start_piece(0)
    q_ring.start_piece(1)
    q_ring.twin(0).start()
    to_head(o_v, got_o, oa_send, oa_recv, peers)
    to_self(o_v, got_o, oa_recv)

    for load in loads[6:]:
        load.wait()

    def probs(par, k):
        s = lax.dot_general(kx[...], qb[par, k, pl.ds(0, rows), :], NT, preferred_element_type=jnp.float32)
        lse_tile = qb[par, k, pl.ds(rows + 16 * tiles, 16), :].astype(jnp.float32)
        biases = []
        block = lax.broadcasted_iota(jnp.int32, (per_shard, 128), 0)
        for t in range(tiles):
            rel = qb[par, k, pl.ds(rows + 16 * t, 16), :].astype(jnp.float32).astype(jnp.int32) - own * per_shard
            bits = jnp.where((rel >= 0) & (rel < per_shard), jnp.left_shift(1, jnp.maximum(jnp.minimum(rel, per_shard), 0)), 0)
            bits = jnp.sum(bits, axis=0, keepdims=True)
            named = jnp.right_shift(jnp.broadcast_to(bits, (per_shard, 128)), block) & 1
            biases.append(jnp.where(named == 1, jnp.broadcast_to(lse_tile[t : t + 1, :] * -LOG2E, (per_shard, 128)), -1e30))
        bias = jnp.concatenate(biases, axis=1)
        for b in range(per_shard):
            pt[par, k, pl.ds(b * BLK, BLK), :] = jnp.exp2(
                s[b * BLK : (b + 1) * BLK, :] * (scale * LOG2E) + bias[b : b + 1, :]
            )

    def give(k):
        return pltpu.make_async_remote_copy(
            src_ref=part.at[1, k],
            dst_ref=pr.at[k],
            send_sem=p_send.at[k],
            recv_sem=p_recv.at[k],
            device_id=sib,
        )

    def score_grads(par, k):
        g = gb[par, k, pl.ds(0, rows), :]
        tile = gb[par, k, pl.ds(rows, 16), :].astype(jnp.float32)
        delta = jnp.concatenate([tile[t : t + 1, :] for t in range(tiles)], axis=1)
        dp = lax.dot_general(vx[...], g, NT, preferred_element_type=jnp.float32)
        p = pt[par, k]
        ds = (p * (dp - delta)).astype(jnp.bfloat16)
        part[par, k] = jnp.dot(kt[...], ds, preferred_element_type=jnp.float32)
        return p.astype(jnp.bfloat16), g, ds, qb[par, k, pl.ds(0, rows), :]

    def grads(first, second):
        p, g, ds, q = (jnp.concatenate(both, axis=i) for both, i in zip(zip(score_grads(*first), score_grads(*second)), (1, 0, 1, 0)))
        dv_acc[...] += jnp.dot(p, g, preferred_element_type=jnp.float32)
        dk_acc[...] += jnp.dot(ds, q, preferred_element_type=jnp.float32)

    def backward_pair(d, par):
        single = (d == 0) | (d == 4)
        par1 = jnp.where(single, 0, par)
        par2 = jnp.where(single, 1, par)
        k2 = jnp.where(single, d, RING - d)

        @pl.when(par1 == 1)
        def _():
            g_ring.twin(d).wait_recv()

        @pl.when(par2 == 1)
        def _():
            g_ring.twin(k2).wait_recv()

        grads((par1, d), (par2, k2))

        @pl.when(par1 == 1)
        def _():
            give(d).start()

        @pl.when(par2 == 1)
        def _():
            give(k2).start()

    def visit(d, par, side, rings, compute):
        k = jnp.where(side == 0, d, (RING - d) % RING)

        @pl.when(((side == 0) & (d >= 0) & (d <= 4)) | ((d >= 1) & (d < 4)))
        def _():
            @pl.when(par == 1)
            def _():
                for ring in rings:
                    ring.twin(k).wait_recv()

            compute(par, k)

    width = dh // CHAIN

    def chain(side, d, h):
        return pltpu.make_async_remote_copy(
            src_ref=sl.at[side, d, h],
            dst_ref=rl.at[side, d - 1, h],
            send_sem=c_send.at[side, d, h],
            recv_sem=c_recv.at[side, d - 1, h],
            device_id=dirs[1 - side],
        )

    def far(side):
        return pltpu.make_async_remote_copy(
            src_ref=far_s.at[side],
            dst_ref=far_r.at[side],
            send_sem=f_send.at[side],
            recv_sem=f_recv.at[side],
            device_id=far_home[side],
        )

    def local_sum(k, h):
        return part[0, k, pl.ds(h * width, width), :] + pr[k, pl.ds(h * width, width), :]

    def mine_to_take(side, h):
        return (h < CHAIN // 2) == (side == 0)

    def send_home(d):
        for side in range(2):
            give(slot(side, d)).wait_recv()
        for i in range(CHAIN):
            for side in range(2):
                h = (i + (1 - side) * (CHAIN // 2)) % CHAIN
                total = local_sum(slot(side, d), h)
                if d < 3:
                    chain(side, d + 1, h).wait_recv()
                    total = total + rl[side, d, h].astype(jnp.float32)
                if d == 1 and mine_to_take(side, h):
                    if i == CHAIN // 2:
                        far(side).wait_recv()
                    total = total + far_r[side, i - CHAIN // 2].astype(jnp.float32)
                sl[side, d, h] = total.astype(jnp.bfloat16)
                chain(side, d, h).start()

    def tick(t, _):
        @pl.when((t >= 1) & (t <= 4))
        def _():
            q_ring.relay(t)

        def forward(j, _):
            visit(t, j // 2, j % 2, (q_ring,), probs)
            return 0

        @pl.when(t <= 4)
        def _():
            lax.fori_loop(0, 4, forward, 0)

        @pl.when(t == 2)
        def _():
            pltpu.make_async_copy(got_g, got_g, ga_recv).wait()
            g = got_g[...].astype(jnp.float32).reshape(rows, dh)
            gb[0, 0, pl.ds(0, rows), :] = g.astype(jnp.bfloat16)
            g_ring.start_piece(0)
            kt[...] = kx[...].astype(jnp.float32).T.astype(jnp.bfloat16)
            dk_acc[...] = jnp.zeros_like(dk_acc)
            dv_acc[...] = jnp.zeros_like(dv_acc)
            pltpu.make_async_copy(got_o, got_o, oa_recv).wait()
            o = got_o[...].astype(jnp.float32).reshape(rows, dh)
            delta = lax.dot_general(
                jnp.ones((8, dh), jnp.float32), gb[0, 0, pl.ds(0, rows), :].astype(jnp.float32) * o, NT,
                precision=lax.Precision.HIGHEST, preferred_element_type=jnp.float32,
            )
            gb[0, 0, pl.ds(rows, 16), :] = lane_tiles(delta[0:1, :])
            g_ring.start_piece(1)
            g_ring.twin(0).start()

        @pl.when(t >= 3)
        def _():
            g_ring.relay(t - 2)

        def backward(j, _):
            backward_pair(t - 2, j)
            return 0

        @pl.when(t == 6)
        def _():
            send_home(3)

        @pl.when(t >= 2)
        def _():
            lax.fori_loop(0, jnp.where((t == 2) | (t == 6), 1, 2), backward, 0)

        return 0

    lax.fori_loop(0, 7, tick, 0)

    give(4).wait_recv()
    for side in range(2):
        for i in range(CHAIN // 2):
            far_s[side, i] = local_sum(4, side * (CHAIN // 2) + i).astype(jnp.bfloat16)
        far(side).start()

    dk_v[...] = (dk_acc[...] * scale).astype(jnp.bfloat16)
    dv_v[...] = dv_acc[...].astype(jnp.bfloat16)
    stores = [
        pltpu.make_async_copy(dk_v, dk_hbm, out_sem.at[0]),
        pltpu.make_async_copy(dv_v, dv_hbm, out_sem.at[1]),
        pltpu.make_async_copy(dq_v, dq_hbm, out_sem.at[2]),
    ]
    stores[0].start()
    stores[1].start()

    send_home(2)
    send_home(1)
    give(0).wait_recv()
    totals = []
    for h in range(CHAIN):
        total = local_sum(0, h)
        for side in range(2):
            chain(side, 1, h).wait_recv()
            total = total + rl[side, 0, h].astype(jnp.float32)
        totals.append(total)
    dq_v[...] = (jnp.concatenate(totals, axis=0) * scale).T.astype(jnp.bfloat16)
    stores[2].start()

    q_ring.drain()
    g_ring.drain()

    def given(k, _):
        give(k).wait_send()
        return 0

    lax.fori_loop(0, RING, given, 0)
    for side in range(2):
        far(side).wait_send()
        for d in range(1, 4):
            for h in range(CHAIN):
                chain(side, d, h).wait_send()
    if n_head > 1:
        for got, sem in ((got_g, ga_send), (got_o, oa_send)):
            others = got.at[pl.ds(0, n_head - 1)]
            pltpu.make_async_copy(others, others, sem).wait()
    for store in stores:
        store.wait()


def local(query_rows, key_rows, value_rows, attn_out, out_grad, logsumexp, shard_pick, block_pick):
    n_head = lax.axis_size("head")
    rows, dh = query_rows.shape
    keys = key_rows.shape[0]
    r = rows // n_head
    tiles = rows // 128
    q_rows = rows + 16 * tiles + 16
    groups, per_group = block_pick.shape[2:]
    bf, f32 = jnp.bfloat16, jnp.float32
    dma = pltpu.SemaphoreType.DMA
    vm = pltpu.VMEM
    return pl.pallas_call(
        functools.partial(kernel, n_head),
        out_shape=(
            jax.ShapeDtypeStruct((rows, dh), bf),
            jax.ShapeDtypeStruct((keys, dh), bf),
            jax.ShapeDtypeStruct((keys, dh), bf),
        ),
        in_specs=[pl.BlockSpec(memory_space=pl.ANY)] * 8,
        out_specs=(pl.BlockSpec(memory_space=pl.ANY),) * 3,
        scratch_shapes=[
            vm((2, RING, q_rows, dh), bf),
            vm((2, RING, rows + 16, dh), bf),
            vm((keys, dh), bf),
            vm((keys, dh), bf),
            vm((dh, keys), bf),
            vm((r, n_head * dh), bf),
            vm((r, n_head * dh), bf),
            vm((1, rows), bf),
            vm((groups, rows), jnp.int32),
            vm((groups, per_group, rows), jnp.int32),
            vm((n_head, r, dh), bf),
            vm((n_head, r, dh), bf),
            vm((2, RING, keys, rows), f32),
            vm((2, RING, dh, rows), f32),
            vm((RING, dh, rows), f32),
            vm((2, 4, CHAIN, dh // CHAIN, rows), bf),
            vm((2, 3, CHAIN, dh // CHAIN, rows), bf),
            vm((2, CHAIN // 2, dh // CHAIN, rows), bf),
            vm((2, CHAIN // 2, dh // CHAIN, rows), bf),
            vm((keys, dh), f32),
            vm((keys, dh), f32),
            vm((rows, dh), bf),
            vm((keys, dh), bf),
            vm((keys, dh), bf),
            dma((8,)),
            dma, dma, dma, dma,
            dma((2, 4, 2)), dma((2, 5, 2)), dma((RING,)), dma((RING,)),
            dma((2, 4, 2)), dma((2, 5, 2)), dma((RING,)), dma((RING,)),
            dma((RING,)), dma((RING,)), dma((2, 4, CHAIN)), dma((2, 3, CHAIN)),
            dma((2,)), dma((2,)), dma((3,)),
        ],
        compiler_params=pltpu.CompilerParams(
            collective_id=0, has_side_effects=True, vmem_limit_bytes=56 << 20
        ),
        name="sparse_bwd",
    )(
        query_rows, key_rows, value_rows, attn_out, out_grad, logsumexp,
        shard_pick[0].T, block_pick[0].transpose(1, 2, 0),
    )


def solution(mesh):
    placed = (
        P("seq", "head"),
        P("seq", "head"),
        P("seq", "head"),
        P(("seq", "head"), None),
        P(("seq", "head"), None),
        P("head", "seq"),
        P("head", "seq", None),
        P("head", "seq", None, None),
    )
    return jax.shard_map(
        local,
        mesh=mesh,
        in_specs=placed,
        out_specs=(P("seq", "head"), P("seq", "head"), P("seq", "head")),
        check_vma=False,
    )
```

```python
import functools
import math

import jax
import jax.numpy as jnp
from jax import lax
from jax.experimental import pallas as pl
from jax.experimental.pallas import tpu as pltpu
from jax.sharding import PartitionSpec as P

BLK = 64
RING = 8
HEAD_Z = 12
CHAIN = 4
LOG2E = math.log2(math.e)
NT = (((1,), (1,)), ((), ()))


def kernel(
    n_head, q_hbm, k_hbm, v_hbm, o_hbm, g_hbm, lse_hbm, sp_hbm, bp_hbm,
    dq_hbm, dk_hbm, dv_hbm,
    qb, gb, kx, vx, kt, o_v, g_v, lse_v, sp_v, bp_v, got_g, got_o,
    pt, part, pr, sl, rl, far_s, far_r, dk_acc, dv_acc, dq_v, dk_v, dv_v,
    in_sem, ga_send, ga_recv, oa_send, oa_recv,
    q_send, q_recv, q_ssend, q_srecv,
    g_send, g_recv, g_ssend, g_srecv,
    p_send, p_recv, c_send, c_recv, f_send, f_recv, out_sem,
):
    rows, dh = q_hbm.shape
    tiles = rows // 128
    per_shard = kx.shape[0] // BLK
    r = rows // n_head
    own = lax.axis_index("seq")
    head = lax.axis_index("head")
    chip, core = own // 2, own % 2

    def at_chip(offset):
        return {"seq": ((chip + offset + RING) % RING) * 2 + core}

    right, left = at_chip(1), at_chip(-1)
    sib = {"seq": chip * 2 + (1 - core)}
    dirs = (right, left)
    far_home = (at_chip(-3), at_chip(3))
    scale = dh ** (-0.5)

    zn = HEAD_Z if n_head % HEAD_Z == 0 else n_head
    xn = n_head // zn

    my_x, my_z = head // zn, head % zn

    def away(n, i):
        m = (i + 1) // 2
        return (n // 2 + (2 * (i % 2) - 1) * m + n) % n

    def moved(at, by, n):
        if by == 0:
            return at
        at = at + by
        return jnp.where(at >= n, at - n, at)

    peer_z = [moved(my_z, away(zn, i), zn) for i in range(zn)]
    peer_x = [moved(my_x, away(xn, i), xn) * zn for i in range(xn)]
    peers = [x + z for z in peer_z for x in peer_x][: n_head - 1]

    barrier = pltpu.get_barrier_semaphore()
    for peer in peers:
        pl.semaphore_signal(barrier, inc=1, device_id={"head": peer})
    for peer in (right, left, sib) + far_home:
        pl.semaphore_signal(barrier, inc=1, device_id=peer)

    loads = [
        pltpu.make_async_copy(src, dst, in_sem.at[i])
        for i, (src, dst) in enumerate(
            (
                (q_hbm, qb.at[0, 0, pl.ds(0, rows)]),
                (lse_hbm, lse_v),
                (sp_hbm, sp_v),
                (bp_hbm, bp_v),
                (g_hbm, g_v),
                (o_hbm, o_v),
                (k_hbm, kx),
                (v_hbm, vx),
            )
        )
    ]
    for load in loads:
        load.start()

    for load in loads[:4]:
        load.wait()

    lse = lse_v[...].astype(jnp.float32)
    for t in range(tiles):
        cols = pl.ds(t * 128, 128)
        ids = [sp_v[g : g + 1, cols] * per_shard + bp_v[g, :, cols] for g in range(sp_v.shape[0])]
        ids = jnp.concatenate(ids, axis=0).astype(jnp.float32).astype(jnp.bfloat16)
        qb[0, 0, pl.ds(rows + 16 * t, 16), :] = ids
    sub = lax.broadcasted_iota(jnp.int32, (16, 128), 0)

    def lane_tiles(vec):
        out = jnp.broadcast_to(vec[:, 0:128], (16, 128))
        for t in range(1, tiles):
            out = jnp.where(sub == t, jnp.broadcast_to(vec[:, t * 128 : (t + 1) * 128], (16, 128)), out)
        return out.astype(jnp.bfloat16)

    qb[0, 0, pl.ds(rows + 16 * tiles, 16), :] = lane_tiles(lse)
    for load in loads[4:6]:
        load.wait()

    def slot(side, d):
        return d if side == 0 else (RING - d) % RING

    class Ring:
        def __init__(self, buf, cut, send, recv, ssend, srecv):
            self.buf = buf
            self.spans = (pl.ds(0, cut), pl.ds(cut, buf.shape[2] - cut))
            self.send, self.recv, self.ssend, self.srecv = send, recv, ssend, srecv

        def hop(self, side, d, h):
            return pltpu.make_async_remote_copy(
                src_ref=self.buf.at[0, slot(side, d), self.spans[h]],
                dst_ref=self.buf.at[0, slot(side, d + 1), self.spans[h]],
                send_sem=self.send.at[side, d, h],
                recv_sem=self.recv.at[side, d + 1, h],
                device_id=dirs[side],
            )

        def twin(self, k):
            return pltpu.make_async_remote_copy(
                src_ref=self.buf.at[0, k],
                dst_ref=self.buf.at[1, k],
                send_sem=self.ssend.at[k],
                recv_sem=self.srecv.at[k],
                device_id=sib,
            )

        def start_piece(self, h):
            for side in range(2):
                self.hop(side, 0, h).start()

        def relay(self, d):
            for h in range(2):
                for side in range(2):
                    @pl.when((d < 4) | (h == side))
                    def _():
                        self.hop(side, d - 1, h).wait_recv()

                    @pl.when((d < 3) | ((d == 3) & (h == side)))
                    def _():
                        self.hop(side, d, h).start()

            self.twin(d).start()

            @pl.when(d < 4)
            def _():
                self.twin(RING - d).start()

        def drain(self):
            def per_hop(d, _):
                for h in range(2):
                    for side in range(2):
                        @pl.when((d < 3) | (h == side))
                        def _():
                            self.hop(side, d, h).wait_send()
                return 0

            lax.fori_loop(0, 4, per_hop, 0)

            def per_slot(k, _):
                self.twin(k).wait_send()
                return 0

            lax.fori_loop(0, RING, per_slot, 0)

    q_ring = Ring(qb, qb.shape[2] // 2, q_send, q_recv, q_ssend, q_srecv)
    g_ring = Ring(gb, rows // 2, g_send, g_recv, g_ssend, g_srecv)

    def to_head(src, dst, send, recv, some):
        for peer in some:
            pltpu.make_async_remote_copy(
                src_ref=src.at[:, pl.ds(pl.multiple_of(peer * dh, dh), dh)],
                dst_ref=dst.at[head],
                send_sem=send,
                recv_sem=recv,
                device_id={"head": peer},
            ).start()

    def to_self(src, dst, recv):
        mine = src.at[:, pl.ds(pl.multiple_of(head * dh, dh), dh)]
        pltpu.make_async_copy(mine, dst.at[head], recv).start()

    pl.semaphore_wait(barrier, n_head - 1 + 5)
    to_head(g_v, got_g, ga_send, ga_recv, peers)
    to_self(g_v, got_g, ga_recv)
    q_ring.start_piece(0)
    q_ring.start_piece(1)
    q_ring.twin(0).start()
    to_head(o_v, got_o, oa_send, oa_recv, peers)
    to_self(o_v, got_o, oa_recv)

    for load in loads[6:]:
        load.wait()

    def probs(par, k):
        s = lax.dot_general(kx[...], qb[par, k, pl.ds(0, rows), :], NT, preferred_element_type=jnp.float32)
        lse_tile = qb[par, k, pl.ds(rows + 16 * tiles, 16), :].astype(jnp.float32)
        biases = []
        block = lax.broadcasted_iota(jnp.int32, (per_shard, 128), 0)
        for t in range(tiles):
            rel = qb[par, k, pl.ds(rows + 16 * t, 16), :].astype(jnp.float32).astype(jnp.int32) - own * per_shard
            bits = jnp.where((rel >= 0) & (rel < per_shard), jnp.left_shift(1, jnp.maximum(jnp.minimum(rel, per_shard), 0)), 0)
            bits = jnp.sum(bits, axis=0, keepdims=True)
            named = jnp.right_shift(jnp.broadcast_to(bits, (per_shard, 128)), block) & 1
            biases.append(jnp.where(named == 1, jnp.broadcast_to(lse_tile[t : t + 1, :] * -LOG2E, (per_shard, 128)), -1e30))
        bias = jnp.concatenate(biases, axis=1)
        for b in range(per_shard):
            pt[par, k, pl.ds(b * BLK, BLK), :] = jnp.exp2(
                s[b * BLK : (b + 1) * BLK, :] * (scale * LOG2E) + bias[b : b + 1, :]
            )

    def give(k):
        return pltpu.make_async_remote_copy(
            src_ref=part.at[1, k],
            dst_ref=pr.at[k],
            send_sem=p_send.at[k],
            recv_sem=p_recv.at[k],
            device_id=sib,
        )

    def score_grads(par, k):
        g = gb[par, k, pl.ds(0, rows), :]
        tile = gb[par, k, pl.ds(rows, 16), :].astype(jnp.float32)
        delta = jnp.concatenate([tile[t : t + 1, :] for t in range(tiles)], axis=1)
        dp = lax.dot_general(vx[...], g, NT, preferred_element_type=jnp.float32)
        p = pt[par, k]
        ds = (p * (dp - delta)).astype(jnp.bfloat16)
        part[par, k] = jnp.dot(kt[...], ds, preferred_element_type=jnp.float32)
        return p.astype(jnp.bfloat16), g, ds, qb[par, k, pl.ds(0, rows), :]

    def grads(first, second):
        p, g, ds, q = (jnp.concatenate(both, axis=i) for both, i in zip(zip(score_grads(*first), score_grads(*second)), (1, 0, 1, 0)))
        dv_acc[...] += jnp.dot(p, g, preferred_element_type=jnp.float32)
        dk_acc[...] += jnp.dot(ds, q, preferred_element_type=jnp.float32)

    def backward_pair(d, par):
        single = (d == 0) | (d == 4)
        par1 = jnp.where(single, 0, par)
        par2 = jnp.where(single, 1, par)
        k2 = jnp.where(single, d, RING - d)

        @pl.when(par1 == 1)
        def _():
            g_ring.twin(d).wait_recv()

        @pl.when(par2 == 1)
        def _():
            g_ring.twin(k2).wait_recv()

        grads((par1, d), (par2, k2))

        @pl.when(par1 == 1)
        def _():
            give(d).start()

        @pl.when(par2 == 1)
        def _():
            give(k2).start()

    def visit(d, par, side, rings, compute):
        k = jnp.where(side == 0, d, (RING - d) % RING)

        @pl.when(((side == 0) & (d >= 0) & (d <= 4)) | ((d >= 1) & (d < 4)))
        def _():
            @pl.when(par == 1)
            def _():
                for ring in rings:
                    ring.twin(k).wait_recv()

            compute(par, k)

    width = dh // CHAIN

    def chain(side, d, h):
        return pltpu.make_async_remote_copy(
            src_ref=sl.at[side, d, h],
            dst_ref=rl.at[side, d - 1, h],
            send_sem=c_send.at[side, d, h],
            recv_sem=c_recv.at[side, d - 1, h],
            device_id=dirs[1 - side],
        )

    def far(side):
        return pltpu.make_async_remote_copy(
            src_ref=far_s.at[side],
            dst_ref=far_r.at[side],
            send_sem=f_send.at[side],
            recv_sem=f_recv.at[side],
            device_id=far_home[side],
        )

    def local_sum(k, h):
        return part[0, k, pl.ds(h * width, width), :] + pr[k, pl.ds(h * width, width), :]

    def mine_to_take(side, h):
        return (h < CHAIN // 2) == (side == 0)

    def send_home(d):
        for side in range(2):
            give(slot(side, d)).wait_recv()
        for i in range(CHAIN):
            for side in range(2):
                h = (i + (1 - side) * (CHAIN // 2)) % CHAIN
                total = local_sum(slot(side, d), h)
                if d < 3:
                    chain(side, d + 1, h).wait_recv()
                    total = total + rl[side, d, h].astype(jnp.float32)
                if d == 1 and mine_to_take(side, h):
                    if i == CHAIN // 2:
                        far(side).wait_recv()
                    total = total + far_r[side, i - CHAIN // 2].astype(jnp.float32)
                sl[side, d, h] = total.astype(jnp.bfloat16)
                chain(side, d, h).start()

    def tick(t, _):
        @pl.when((t >= 1) & (t <= 4))
        def _():
            q_ring.relay(t)

        @pl.when(t == 2)
        def _():
            pltpu.make_async_copy(got_g, got_g, ga_recv).wait()
            g = got_g[...].astype(jnp.float32).reshape(rows, dh)
            gb[0, 0, pl.ds(0, rows), :] = g.astype(jnp.bfloat16)
            g_ring.start_piece(0)
            kt[...] = kx[...].astype(jnp.float32).T.astype(jnp.bfloat16)
            dk_acc[...] = jnp.zeros_like(dk_acc)
            dv_acc[...] = jnp.zeros_like(dv_acc)

        def forward(j, _):
            visit(t, j // 2, j % 2, (q_ring,), probs)
            return 0

        @pl.when(t <= 4)
        def _():
            lax.fori_loop(0, 4, forward, 0)

        @pl.when(t == 2)
        def _():
            pltpu.make_async_copy(got_o, got_o, oa_recv).wait()
            o = got_o[...].astype(jnp.float32).reshape(rows, dh)
            delta = lax.dot_general(
                jnp.ones((8, dh), jnp.float32), gb[0, 0, pl.ds(0, rows), :].astype(jnp.float32) * o, NT,
                precision=lax.Precision.HIGHEST, preferred_element_type=jnp.float32,
            )
            gb[0, 0, pl.ds(rows, 16), :] = lane_tiles(delta[0:1, :])
            g_ring.start_piece(1)
            g_ring.twin(0).start()

        @pl.when(t >= 3)
        def _():
            g_ring.relay(t - 2)

        def backward(j, _):
            backward_pair(t - 2, j)
            return 0

        @pl.when(t == 6)
        def _():
            send_home(3)

        @pl.when(t >= 2)
        def _():
            lax.fori_loop(0, jnp.where((t == 2) | (t == 6), 1, 2), backward, 0)

        return 0

    lax.fori_loop(0, 7, tick, 0)

    give(4).wait_recv()
    for side in range(2):
        for i in range(CHAIN // 2):
            far_s[side, i] = local_sum(4, side * (CHAIN // 2) + i).astype(jnp.bfloat16)
        far(side).start()

    dk_v[...] = (dk_acc[...] * scale).astype(jnp.bfloat16)
    dv_v[...] = dv_acc[...].astype(jnp.bfloat16)
    stores = [
        pltpu.make_async_copy(dk_v, dk_hbm, out_sem.at[0]),
        pltpu.make_async_copy(dv_v, dv_hbm, out_sem.at[1]),
        pltpu.make_async_copy(dq_v, dq_hbm, out_sem.at[2]),
    ]
    stores[0].start()
    stores[1].start()

    q_ring.drain()
    g_ring.drain()

    def given(k, _):
        give(k).wait_send()
        return 0

    lax.fori_loop(0, RING, given, 0)
    if n_head > 1:
        for got, sem in ((got_g, ga_send), (got_o, oa_send)):
            others = got.at[pl.ds(0, n_head - 1)]
            pltpu.make_async_copy(others, others, sem).wait()

    send_home(2)
    send_home(1)
    give(0).wait_recv()
    totals = []
    for h in range(CHAIN):
        total = local_sum(0, h)
        for side in range(2):
            chain(side, 1, h).wait_recv()
            total = total + rl[side, 0, h].astype(jnp.float32)
        totals.append(total)
    dq_v[...] = (jnp.concatenate(totals, axis=0) * scale).T.astype(jnp.bfloat16)
    stores[2].start()

    for side in range(2):
        far(side).wait_send()
        for d in range(1, 4):
            for h in range(CHAIN):
                chain(side, d, h).wait_send()
    for store in stores:
        store.wait()


def local(query_rows, key_rows, value_rows, attn_out, out_grad, logsumexp, shard_pick, block_pick):
    n_head = lax.axis_size("head")
    rows, dh = query_rows.shape
    keys = key_rows.shape[0]
    r = rows // n_head
    tiles = rows // 128
    q_rows = rows + 16 * tiles + 16
    groups, per_group = block_pick.shape[2:]
    bf, f32 = jnp.bfloat16, jnp.float32
    dma = pltpu.SemaphoreType.DMA
    vm = pltpu.VMEM
    return pl.pallas_call(
        functools.partial(kernel, n_head),
        out_shape=(
            jax.ShapeDtypeStruct((rows, dh), bf),
            jax.ShapeDtypeStruct((keys, dh), bf),
            jax.ShapeDtypeStruct((keys, dh), bf),
        ),
        in_specs=[pl.BlockSpec(memory_space=pl.ANY)] * 8,
        out_specs=(pl.BlockSpec(memory_space=pl.ANY),) * 3,
        scratch_shapes=[
            vm((2, RING, q_rows, dh), bf),
            vm((2, RING, rows + 16, dh), bf),
            vm((keys, dh), bf),
            vm((keys, dh), bf),
            vm((dh, keys), bf),
            vm((r, n_head * dh), bf),
            vm((r, n_head * dh), bf),
            vm((1, rows), bf),
            vm((groups, rows), jnp.int32),
            vm((groups, per_group, rows), jnp.int32),
            vm((n_head, r, dh), bf),
            vm((n_head, r, dh), bf),
            vm((2, RING, keys, rows), f32),
            vm((2, RING, dh, rows), f32),
            vm((RING, dh, rows), f32),
            vm((2, 4, CHAIN, dh // CHAIN, rows), bf),
            vm((2, 3, CHAIN, dh // CHAIN, rows), bf),
            vm((2, CHAIN // 2, dh // CHAIN, rows), bf),
            vm((2, CHAIN // 2, dh // CHAIN, rows), bf),
            vm((keys, dh), f32),
            vm((keys, dh), f32),
            vm((rows, dh), bf),
            vm((keys, dh), bf),
            vm((keys, dh), bf),
            dma((8,)),
            dma, dma, dma, dma,
            dma((2, 4, 2)), dma((2, 5, 2)), dma((RING,)), dma((RING,)),
            dma((2, 4, 2)), dma((2, 5, 2)), dma((RING,)), dma((RING,)),
            dma((RING,)), dma((RING,)), dma((2, 4, CHAIN)), dma((2, 3, CHAIN)),
            dma((2,)), dma((2,)), dma((3,)),
        ],
        compiler_params=pltpu.CompilerParams(
            collective_id=0, has_side_effects=True, vmem_limit_bytes=56 << 20
        ),
        name="sparse_bwd",
    )(
        query_rows, key_rows, value_rows, attn_out, out_grad, logsumexp,
        shard_pick[0].T, block_pick[0].transpose(1, 2, 0),
    )


def solution(mesh):
    placed = (
        P("seq", "head"),
        P("seq", "head"),
        P("seq", "head"),
        P(("seq", "head"), None),
        P(("seq", "head"), None),
        P("head", "seq"),
        P("head", "seq", None),
        P("head", "seq", None, None),
    )
    return jax.shard_map(
        local,
        mesh=mesh,
        in_specs=placed,
        out_specs=(P("seq", "head"), P("seq", "head"), P("seq", "head")),
        check_vma=False,
    )
```

```python
import functools
import math

import jax
import jax.numpy as jnp
from jax import lax
from jax.experimental import pallas as pl
from jax.experimental.pallas import tpu as pltpu
from jax.sharding import PartitionSpec as P

BLK = 64
RING = 8
HEAD_Z = 12
CHAIN = 4
LOG2E = math.log2(math.e)
NT = (((1,), (1,)), ((), ()))


def kernel(
    n_head, q_hbm, k_hbm, v_hbm, o_hbm, g_hbm, lse_hbm, sp_hbm, bp_hbm,
    dq_hbm, dk_hbm, dv_hbm,
    qb, gb, kx, vx, kt, o_v, g_v, lse_v, sp_v, bp_v, got_g, got_o,
    pt, part, pr, sl, rl, far_s, far_r, dk_acc, dv_acc, dq_v, dk_v, dv_v,
    in_sem, ga_send, ga_recv, oa_send, oa_recv,
    q_send, q_recv, q_ssend, q_srecv,
    g_send, g_recv, g_ssend, g_srecv,
    p_send, p_recv, c_send, c_recv, f_send, f_recv, out_sem,
):
    rows, dh = q_hbm.shape
    tiles = rows // 128
    per_shard = kx.shape[0] // BLK
    r = rows // n_head
    own = lax.axis_index("seq")
    head = lax.axis_index("head")
    chip, core = own // 2, own % 2

    def at_chip(offset):
        return {"seq": ((chip + offset + RING) % RING) * 2 + core}

    right, left = at_chip(1), at_chip(-1)
    sib = {"seq": chip * 2 + (1 - core)}
    dirs = (right, left)
    far_home = (at_chip(-3), at_chip(3))
    scale = dh ** (-0.5)

    zn = HEAD_Z if n_head % HEAD_Z == 0 else n_head
    xn = n_head // zn

    my_x, my_z = head // zn, head % zn

    def away(n, i):
        m = (i + 1) // 2
        return (n // 2 + (2 * (i % 2) - 1) * m + n) % n

    def moved(at, by, n):
        if by == 0:
            return at
        at = at + by
        return jnp.where(at >= n, at - n, at)

    peer_z = [moved(my_z, away(zn, i), zn) for i in range(zn)]
    peer_x = [moved(my_x, away(xn, i), xn) * zn for i in range(xn)]
    peers = [x + z for z in peer_z for x in peer_x][: n_head - 1]

    barrier = pltpu.get_barrier_semaphore()
    for peer in peers:
        pl.semaphore_signal(barrier, inc=1, device_id={"head": peer})
    for peer in (right, left, sib) + far_home:
        pl.semaphore_signal(barrier, inc=1, device_id=peer)

    loads = [
        pltpu.make_async_copy(src, dst, in_sem.at[i])
        for i, (src, dst) in enumerate(
            (
                (q_hbm, qb.at[0, 0, pl.ds(0, rows)]),
                (lse_hbm, lse_v),
                (sp_hbm, sp_v),
                (bp_hbm, bp_v),
                (g_hbm, g_v),
                (o_hbm, o_v),
                (k_hbm, kx),
                (v_hbm, vx),
            )
        )
    ]
    for load in loads:
        load.start()

    for load in loads[:4]:
        load.wait()

    lse = lse_v[...].astype(jnp.float32)
    for t in range(tiles):
        cols = pl.ds(t * 128, 128)
        ids = [sp_v[g : g + 1, cols] * per_shard + bp_v[g, :, cols] for g in range(sp_v.shape[0])]
        ids = jnp.concatenate(ids, axis=0).astype(jnp.float32).astype(jnp.bfloat16)
        qb[0, 0, pl.ds(rows + 16 * t, 16), :] = ids
    sub = lax.broadcasted_iota(jnp.int32, (16, 128), 0)

    def lane_tiles(vec):
        out = jnp.broadcast_to(vec[:, 0:128], (16, 128))
        for t in range(1, tiles):
            out = jnp.where(sub == t, jnp.broadcast_to(vec[:, t * 128 : (t + 1) * 128], (16, 128)), out)
        return out.astype(jnp.bfloat16)

    qb[0, 0, pl.ds(rows + 16 * tiles, 16), :] = lane_tiles(lse)
    for load in loads[4:6]:
        load.wait()

    def slot(side, d):
        return d if side == 0 else (RING - d) % RING

    class Ring:
        def __init__(self, buf, cut, send, recv, ssend, srecv):
            self.buf = buf
            self.spans = (pl.ds(0, cut), pl.ds(cut, buf.shape[2] - cut))
            self.send, self.recv, self.ssend, self.srecv = send, recv, ssend, srecv

        def hop(self, side, d, h):
            return pltpu.make_async_remote_copy(
                src_ref=self.buf.at[0, slot(side, d), self.spans[h]],
                dst_ref=self.buf.at[0, slot(side, d + 1), self.spans[h]],
                send_sem=self.send.at[side, d, h],
                recv_sem=self.recv.at[side, d + 1, h],
                device_id=dirs[side],
            )

        def twin(self, k):
            return pltpu.make_async_remote_copy(
                src_ref=self.buf.at[0, k],
                dst_ref=self.buf.at[1, k],
                send_sem=self.ssend.at[k],
                recv_sem=self.srecv.at[k],
                device_id=sib,
            )

        def start_piece(self, h):
            for side in range(2):
                self.hop(side, 0, h).start()

        def relay(self, d):
            for h in range(2):
                for side in range(2):
                    @pl.when((d < 4) | (h == side))
                    def _():
                        self.hop(side, d - 1, h).wait_recv()

                    @pl.when((d < 3) | ((d == 3) & (h == side)))
                    def _():
                        self.hop(side, d, h).start()

            self.twin(d).start()

            @pl.when(d < 4)
            def _():
                self.twin(RING - d).start()

        def leap(self, side):
            return pltpu.make_async_remote_copy(
                src_ref=self.buf.at[0, 0, self.spans[side]],
                dst_ref=self.buf.at[0, slot(side, 3), self.spans[side]],
                send_sem=self.send.at[side, 2, side],
                recv_sem=self.recv.at[side, 3, side],
                device_id=far_home[1 - side],
            )

        def relay_rest(self, d):
            for h in range(2):
                for side in range(2):
                    last = 2 if h == side else 3

                    @pl.when(d <= last)
                    def _():
                        self.hop(side, d - 1, h).wait_recv()

                    @pl.when(d < last)
                    def _():
                        self.hop(side, d, h).start()

            self.twin(d).start()
            self.twin(RING - d).start()

        def drain(self):
            def per_hop(d, _):
                for h in range(2):
                    for side in range(2):
                        @pl.when((d < 3) | (h == side))
                        def _():
                            self.hop(side, d, h).wait_send()
                return 0

            lax.fori_loop(0, 4, per_hop, 0)

            def per_slot(k, _):
                self.twin(k).wait_send()
                return 0

            lax.fori_loop(0, RING, per_slot, 0)

    q_ring = Ring(qb, qb.shape[2] // 2, q_send, q_recv, q_ssend, q_srecv)
    g_ring = Ring(gb, rows // 2, g_send, g_recv, g_ssend, g_srecv)

    def to_head(src, dst, send, recv, some):
        for peer in some:
            pltpu.make_async_remote_copy(
                src_ref=src.at[:, pl.ds(pl.multiple_of(peer * dh, dh), dh)],
                dst_ref=dst.at[head],
                send_sem=send,
                recv_sem=recv,
                device_id={"head": peer},
            ).start()

    def to_self(src, dst, recv):
        mine = src.at[:, pl.ds(pl.multiple_of(head * dh, dh), dh)]
        pltpu.make_async_copy(mine, dst.at[head], recv).start()

    pl.semaphore_wait(barrier, n_head - 1 + 5)
    to_head(g_v, got_g, ga_send, ga_recv, peers)
    to_self(g_v, got_g, ga_recv)
    q_ring.start_piece(0)
    q_ring.start_piece(1)
    q_ring.twin(0).start()
    to_head(o_v, got_o, oa_send, oa_recv, peers)
    to_self(o_v, got_o, oa_recv)

    for load in loads[6:]:
        load.wait()

    def probs(par, k):
        s = lax.dot_general(kx[...], qb[par, k, pl.ds(0, rows), :], NT, preferred_element_type=jnp.float32)
        lse_tile = qb[par, k, pl.ds(rows + 16 * tiles, 16), :].astype(jnp.float32)
        biases = []
        block = lax.broadcasted_iota(jnp.int32, (per_shard, 128), 0)
        for t in range(tiles):
            rel = qb[par, k, pl.ds(rows + 16 * t, 16), :].astype(jnp.float32).astype(jnp.int32) - own * per_shard
            bits = jnp.where((rel >= 0) & (rel < per_shard), jnp.left_shift(1, jnp.maximum(jnp.minimum(rel, per_shard), 0)), 0)
            bits = jnp.sum(bits, axis=0, keepdims=True)
            named = jnp.right_shift(jnp.broadcast_to(bits, (per_shard, 128)), block) & 1
            biases.append(jnp.where(named == 1, jnp.broadcast_to(lse_tile[t : t + 1, :] * -LOG2E, (per_shard, 128)), -1e30))
        bias = jnp.concatenate(biases, axis=1)
        for b in range(per_shard):
            pt[par, k, pl.ds(b * BLK, BLK), :] = jnp.exp2(
                s[b * BLK : (b + 1) * BLK, :] * (scale * LOG2E) + bias[b : b + 1, :]
            )

    def give(k):
        return pltpu.make_async_remote_copy(
            src_ref=part.at[1, k],
            dst_ref=pr.at[k],
            send_sem=p_send.at[k],
            recv_sem=p_recv.at[k],
            device_id=sib,
        )

    def score_grads(par, k):
        g = gb[par, k, pl.ds(0, rows), :]
        tile = gb[par, k, pl.ds(rows, 16), :].astype(jnp.float32)
        delta = jnp.concatenate([tile[t : t + 1, :] for t in range(tiles)], axis=1)
        dp = lax.dot_general(vx[...], g, NT, preferred_element_type=jnp.float32)
        p = pt[par, k]
        ds = (p * (dp - delta)).astype(jnp.bfloat16)
        part[par, k] = jnp.dot(kt[...], ds, preferred_element_type=jnp.float32)
        return p.astype(jnp.bfloat16), g, ds, qb[par, k, pl.ds(0, rows), :]

    def grads(first, second):
        p, g, ds, q = (jnp.concatenate(both, axis=i) for both, i in zip(zip(score_grads(*first), score_grads(*second)), (1, 0, 1, 0)))
        dv_acc[...] += jnp.dot(p, g, preferred_element_type=jnp.float32)
        dk_acc[...] += jnp.dot(ds, q, preferred_element_type=jnp.float32)

    def backward_pair(d, par):
        single = (d == 0) | (d == 4)
        par1 = jnp.where(single, 0, par)
        par2 = jnp.where(single, 1, par)
        k2 = jnp.where(single, d, RING - d)

        @pl.when(par1 == 1)
        def _():
            g_ring.twin(d).wait_recv()

        @pl.when(par2 == 1)
        def _():
            g_ring.twin(k2).wait_recv()

        grads((par1, d), (par2, k2))

        @pl.when(par1 == 1)
        def _():
            give(d).start()

        @pl.when(par2 == 1)
        def _():
            give(k2).start()

    def visit(d, par, side, rings, compute):
        k = jnp.where(side == 0, d, (RING - d) % RING)

        @pl.when(((side == 0) & (d >= 0) & (d <= 4)) | ((d >= 1) & (d < 4)))
        def _():
            @pl.when(par == 1)
            def _():
                for ring in rings:
                    ring.twin(k).wait_recv()

            compute(par, k)

    width = dh // CHAIN

    def chain(side, d, h):
        return pltpu.make_async_remote_copy(
            src_ref=sl.at[side, d, h],
            dst_ref=rl.at[side, d - 1, h],
            send_sem=c_send.at[side, d, h],
            recv_sem=c_recv.at[side, d - 1, h],
            device_id=dirs[1 - side],
        )

    def far(side):
        return pltpu.make_async_remote_copy(
            src_ref=far_s.at[side],
            dst_ref=far_r.at[side],
            send_sem=f_send.at[side],
            recv_sem=f_recv.at[side],
            device_id=far_home[side],
        )

    def local_sum(k, h):
        return part[0, k, pl.ds(h * width, width), :] + pr[k, pl.ds(h * width, width), :]

    def mine_to_take(side, h):
        return (h < CHAIN // 2) == (side == 0)

    def send_home(d):
        for side in range(2):
            give(slot(side, d)).wait_recv()
        for i in range(CHAIN):
            for side in range(2):
                h = (i + (1 - side) * (CHAIN // 2)) % CHAIN
                total = local_sum(slot(side, d), h)
                if d < 3:
                    chain(side, d + 1, h).wait_recv()
                    total = total + rl[side, d, h].astype(jnp.float32)
                if d == 1 and mine_to_take(side, h):
                    if i == CHAIN // 2:
                        far(side).wait_recv()
                    total = total + far_r[side, i - CHAIN // 2].astype(jnp.float32)
                sl[side, d, h] = total.astype(jnp.bfloat16)
                chain(side, d, h).start()

    def tick(t, _):
        @pl.when((t >= 1) & (t <= 4))
        def _():
            q_ring.relay(t)

        @pl.when(t == 2)
        def _():
            pltpu.make_async_copy(got_g, got_g, ga_recv).wait()
            g = got_g[...].astype(jnp.float32).reshape(rows, dh)
            gb[0, 0, pl.ds(0, rows), :] = g.astype(jnp.bfloat16)
            g_ring.leap(0).start()
            g_ring.start_piece(0)
            kt[...] = kx[...].astype(jnp.float32).T.astype(jnp.bfloat16)
            dk_acc[...] = jnp.zeros_like(dk_acc)
            dv_acc[...] = jnp.zeros_like(dv_acc)

        def forward(j, _):
            visit(t, j // 2, j % 2, (q_ring,), probs)
            return 0

        @pl.when(t <= 4)
        def _():
            lax.fori_loop(0, 4, forward, 0)

        @pl.when(t == 2)
        def _():
            pltpu.make_async_copy(got_o, got_o, oa_recv).wait()
            o = got_o[...].astype(jnp.float32).reshape(rows, dh)
            delta = lax.dot_general(
                jnp.ones((8, dh), jnp.float32), gb[0, 0, pl.ds(0, rows), :].astype(jnp.float32) * o, NT,
                precision=lax.Precision.HIGHEST, preferred_element_type=jnp.float32,
            )
            gb[0, 0, pl.ds(rows, 16), :] = lane_tiles(delta[0:1, :])
            g_ring.leap(1).start()
            g_ring.start_piece(1)
            g_ring.twin(0).start()

        @pl.when(t >= 3)
        def _():
            g_ring.relay_rest(t - 2)

        @pl.when(t == 5)
        def _():
            give(4).wait_recv()
            for side in range(2):
                for i in range(CHAIN // 2):
                    far_s[side, i] = local_sum(4, side * (CHAIN // 2) + i).astype(jnp.bfloat16)
                far(side).start()

        def backward(j, _):
            @pl.when((t == 3) & (j == 1))
            def _():
                for side in range(2):
                    g_ring.leap(side).wait_recv()
                    g_ring.hop(side, 3, side).start()

            @pl.when((t == 4) & (j == 1))
            def _():
                for side in range(2):
                    g_ring.hop(side, 3, side).wait_recv()
                g_ring.twin(4).start()

            backward_pair(jnp.where(j == 2, 4, t - 2), j)
            return 0

        @pl.when(t >= 2)
        def _():
            lax.fori_loop(0, jnp.where(t == 2, 1, jnp.where(t == 4, 3, 2)), backward, 0)

        return 0

    lax.fori_loop(0, 6, tick, 0)

    send_home(3)

    dk_v[...] = (dk_acc[...] * scale).astype(jnp.bfloat16)
    dv_v[...] = dv_acc[...].astype(jnp.bfloat16)
    stores = [
        pltpu.make_async_copy(dk_v, dk_hbm, out_sem.at[0]),
        pltpu.make_async_copy(dv_v, dv_hbm, out_sem.at[1]),
        pltpu.make_async_copy(dq_v, dq_hbm, out_sem.at[2]),
    ]
    stores[0].start()
    stores[1].start()

    q_ring.drain()
    g_ring.drain()

    def given(k, _):
        give(k).wait_send()
        return 0

    lax.fori_loop(0, RING, given, 0)
    if n_head > 1:
        for got, sem in ((got_g, ga_send), (got_o, oa_send)):
            others = got.at[pl.ds(0, n_head - 1)]
            pltpu.make_async_copy(others, others, sem).wait()

    send_home(2)
    send_home(1)
    give(0).wait_recv()
    totals = []
    for h in range(CHAIN):
        total = local_sum(0, h)
        for side in range(2):
            chain(side, 1, h).wait_recv()
            total = total + rl[side, 0, h].astype(jnp.float32)
        totals.append(total)
    dq_v[...] = (jnp.concatenate(totals, axis=0) * scale).T.astype(jnp.bfloat16)
    stores[2].start()

    for side in range(2):
        far(side).wait_send()
        for d in range(1, 4):
            for h in range(CHAIN):
                chain(side, d, h).wait_send()
    for store in stores:
        store.wait()


def local(query_rows, key_rows, value_rows, attn_out, out_grad, logsumexp, shard_pick, block_pick):
    n_head = lax.axis_size("head")
    rows, dh = query_rows.shape
    keys = key_rows.shape[0]
    r = rows // n_head
    tiles = rows // 128
    q_rows = rows + 16 * tiles + 16
    groups, per_group = block_pick.shape[2:]
    bf, f32 = jnp.bfloat16, jnp.float32
    dma = pltpu.SemaphoreType.DMA
    vm = pltpu.VMEM
    return pl.pallas_call(
        functools.partial(kernel, n_head),
        out_shape=(
            jax.ShapeDtypeStruct((rows, dh), bf),
            jax.ShapeDtypeStruct((keys, dh), bf),
            jax.ShapeDtypeStruct((keys, dh), bf),
        ),
        in_specs=[pl.BlockSpec(memory_space=pl.ANY)] * 8,
        out_specs=(pl.BlockSpec(memory_space=pl.ANY),) * 3,
        scratch_shapes=[
            vm((2, RING, q_rows, dh), bf),
            vm((2, RING, rows + 16, dh), bf),
            vm((keys, dh), bf),
            vm((keys, dh), bf),
            vm((dh, keys), bf),
            vm((r, n_head * dh), bf),
            vm((r, n_head * dh), bf),
            vm((1, rows), bf),
            vm((groups, rows), jnp.int32),
            vm((groups, per_group, rows), jnp.int32),
            vm((n_head, r, dh), bf),
            vm((n_head, r, dh), bf),
            vm((2, RING, keys, rows), f32),
            vm((2, RING, dh, rows), f32),
            vm((RING, dh, rows), f32),
            vm((2, 4, CHAIN, dh // CHAIN, rows), bf),
            vm((2, 3, CHAIN, dh // CHAIN, rows), bf),
            vm((2, CHAIN // 2, dh // CHAIN, rows), bf),
            vm((2, CHAIN // 2, dh // CHAIN, rows), bf),
            vm((keys, dh), f32),
            vm((keys, dh), f32),
            vm((rows, dh), bf),
            vm((keys, dh), bf),
            vm((keys, dh), bf),
            dma((8,)),
            dma, dma, dma, dma,
            dma((2, 4, 2)), dma((2, 5, 2)), dma((RING,)), dma((RING,)),
            dma((2, 4, 2)), dma((2, 5, 2)), dma((RING,)), dma((RING,)),
            dma((RING,)), dma((RING,)), dma((2, 4, CHAIN)), dma((2, 3, CHAIN)),
            dma((2,)), dma((2,)), dma((3,)),
        ],
        compiler_params=pltpu.CompilerParams(
            collective_id=0, has_side_effects=True, vmem_limit_bytes=56 << 20
        ),
        name="sparse_bwd",
    )(
        query_rows, key_rows, value_rows, attn_out, out_grad, logsumexp,
        shard_pick[0].T, block_pick[0].transpose(1, 2, 0),
    )


def solution(mesh):
    placed = (
        P("seq", "head"),
        P("seq", "head"),
        P("seq", "head"),
        P(("seq", "head"), None),
        P(("seq", "head"), None),
        P("head", "seq"),
        P("head", "seq", None),
        P("head", "seq", None, None),
    )
    return jax.shard_map(
        local,
        mesh=mesh,
        in_specs=placed,
        out_specs=(P("seq", "head"), P("seq", "head"), P("seq", "head")),
        check_vma=False,
    )
```
